512 devices in a mesh: lat: 64 (over z, y), mem: 8 (over x, core).
Axes of the slice: x: 4, y: 4, z: 16, core: 2. Of those that a mesh axis runs over, the one named last changes fastest.
Arguments:
- ens_perts: bfloat16 [8, 64, 384, 768], P('mem', None, 'lat'), may hold values from -6 to 6
- vert_loc: float32 [64, 64], replicated, may hold values from 0 to 1.8
- lat_lengths: float32 [3], replicated, may hold values from 1.5 to 32
- lon_lengths: float32 [3], replicated, may hold values from 1.5 to 1.7
- scale_weights: float32 [3], replicated, may hold values from 0.3 to 1
- obs_cell: int32 [524288], P('lat'), may hold values from 0 to 294911
- obs_accept: int32 [524288], P('lat'), may hold values 0 or 1
- innovation: float32 [524288], P('lat'), may hold values from -6 to 6
- obs_precision: float32 [524288], P('lat'), may hold values from 0.25 to 4
Outputs:
- new_control: float32 [8, 64, 384, 768], P('mem', None, 'lat')
- gradient: float32 [8, 64, 384, 768], P('mem', None, 'lat')
The draws below stay inside these ranges and needn't reach their ends.
Inputs may be any that keep to these rules, and one draw needn't show every extreme that they name: `obs_cell`: an observation's cell lies in the band of the device that holds it. `obs_accept`: 1 accepts the observation, 0 rejects it.
All inputs are finite; a program needn't handle non-finite values. No bound on the sum of `obs_accept` on one device may be relied on, other than what follows from the above.
Results may differ from the reference program's by a relative error of at most 0.009.
Values may be sent and summed in bfloat16 or wider, within the bound.
A program may use at most 64 MiB of HBM per device.

```python
import math
import jax
import jax.numpy as jnp
from jax import lax

LEV = 64
NY = 384
NX = 768
SCALES = 3
OBS_DEV = 8192
MEMBERS = 8
ROWS_DEV = 6
OBS = 524288


def draw_vert_loc(key, part):
    positions = jnp.arange(LEV, dtype=jnp.float32)
    distance = jnp.abs(positions[:, None] - positions[None, :])
    factor = jax.random.uniform(key, (LEV, LEV), jnp.float32, 0.5, 1.5)
    return jnp.exp(-distance / 30.0) * factor


def with_ends(array, rng, least, largest):
    longest = array.shape.index(max(array.shape))
    spots = []
    for shift in (0, 1):
        where = [jax.random.randint(jax.random.fold_in(rng, axis), (), 0, length) for axis, length in enumerate(array.shape)]
        where[longest] = (where[longest] + shift) % array.shape[longest]
        spots.append(tuple(where))
    return array.at[spots[0]].set(least).at[spots[1]].set(largest)


def levels(key, extent, shards, least, top_value):
    factor_of = 1.0
    for axis_at, blocks in shards:
        heights = jax.random.uniform(jax.random.fold_in(jax.random.fold_in(key, 6), axis_at), (blocks,), jnp.float32, least / len(shards), top_value / len(shards))
        factor_of = factor_of * jnp.repeat(jnp.exp(heights), extent[axis_at] // blocks).reshape((-1,) + (1,) * (len(extent) - 1 - axis_at))
    return factor_of


def centred(own_key, shape, width, reach, shards=(), held_as=jnp.bfloat16):
    drawn = width * jax.random.normal(own_key, shape, jnp.float32)
    if shards:
        drawn = drawn * levels(own_key, shape, shards, -0.22, 0.18)
    return jnp.clip(drawn, -reach, reach).astype(held_as)


def setup_inputs(seed: int = 0) -> dict:
    seeds = jax.random.split(jax.random.key(seed), 10)
    ens_perts = centred(seeds[0], (MEMBERS, LEV, NY, NX), 1.0, 6.0, ((0, 8), (2, 64)))
    vert_loc = draw_vert_loc(jax.random.fold_in(seeds[9], 71), 0)
    lat_lengths = jnp.clip(jnp.exp(jax.random.uniform(seeds[2], (SCALES,), jnp.float32, math.log(1.5), math.log(32.0))), 1.5, 32.0)
    lon_lengths = jnp.clip(jnp.exp(jax.random.uniform(seeds[3], (SCALES,), jnp.float32, math.log(1.5), math.log(1.7))), 1.5, 1.7)
    scale_weights = jnp.clip(jnp.exp(jax.random.uniform(seeds[4], (SCALES,), jnp.float32, math.log(0.3), math.log(1.0))), 0.3, 1.0)
    obs_cell = with_ends(jax.random.randint(seeds[5], (OBS,), 0, LEV * ROWS_DEV * NX), jax.random.fold_in(seeds[5], 1), 0, (LEV * ROWS_DEV * NX) - 1).astype(jnp.int32)
    obs_accept = with_ends((jax.random.randint(seeds[6], (OBS,), 0, 5) < 4).astype(jnp.int32), jax.random.fold_in(seeds[6], 1), 0, 1)
    innovation = centred(seeds[7], (OBS,), 1.0, 6.0, ((0, 64),), jnp.float32)
    obs_precision = jnp.clip(jnp.exp(math.log(4.0) - 2.7725887 * jax.random.uniform(seeds[8], (OBS,), jnp.float32) ** levels(seeds[8], (OBS,), ((0, 64),), -0.2, 0.2)), 0.25, 4.0)
    return dict(ens_perts=ens_perts, vert_loc=vert_loc, lat_lengths=lat_lengths, lon_lengths=lon_lengths, scale_weights=scale_weights, obs_cell=obs_cell, obs_accept=obs_accept, innovation=innovation, obs_precision=obs_precision)


def gaussian_table(lengths, count, periodic):
    positions = jnp.arange(count, dtype=jnp.float32)
    distance = jnp.abs(positions[:, None] - positions[None, :])
    if periodic:
        distance = jnp.minimum(distance, count - distance)
    scaled = distance[None] / lengths[:, None, None]
    return jnp.exp(-0.5 * scaled * scaled).astype(jnp.bfloat16)


def correlate_slab(level_slab, lat_corr, lon_corr, scale_weights):
    summed = jnp.zeros(level_slab.shape, jnp.float32)
    for scale_index in range(SCALES):
        across = jnp.dot(lat_corr[scale_index], level_slab, preferred_element_type=jnp.float32).astype(jnp.bfloat16)
        summed = summed + scale_weights[scale_index] * jnp.dot(across, lon_corr[scale_index], preferred_element_type=jnp.float32)
    return summed.astype(jnp.bfloat16)


def correlate_all(fields, lat_corr, lon_corr, scale_weights):
    flat_fields = fields.reshape(MEMBERS * LEV, NY, NX)
    result = lax.map(lambda level_slab: correlate_slab(level_slab, lat_corr, lon_corr, scale_weights), flat_fields)
    return result.reshape(MEMBERS, LEV, NY, NX)


def reference(ens_perts, vert_loc, lat_lengths, lon_lengths, scale_weights, obs_cell, obs_accept, innovation, obs_precision):
    lat_corr = gaussian_table(lat_lengths, NY, False)
    lon_corr = gaussian_table(lon_lengths, NX, True)
    obs_weight = obs_accept.astype(jnp.float32) * obs_precision
    positions = jnp.arange(OBS, dtype=jnp.int32)
    band_of = positions // OBS_DEV
    obs_level = obs_cell // (ROWS_DEV * NX)
    obs_row = (obs_cell // NX) % ROWS_DEV
    obs_column = obs_cell % NX
    global_cell = (obs_level * NY * NX + (band_of * ROWS_DEV + obs_row) * NX + obs_column).astype(jnp.int32)
    pert_flat = ens_perts.reshape(MEMBERS, LEV * NY * NX)
    pert_at_obs = pert_flat[:, global_cell].astype(jnp.float32)

    def forward(control):
        localized = jnp.einsum("ij,mjrc->mirc", vert_loc, control, precision=lax.Precision.HIGHEST).astype(jnp.bfloat16)
        corr = correlate_all(localized, lat_corr, lon_corr, scale_weights)
        corr_at_obs = corr.reshape(MEMBERS, LEV * NY * NX)[:, global_cell].astype(jnp.float32)
        return jnp.sum(pert_at_obs * corr_at_obs, axis=0)

    def adjoint(obs_values):
        spread = jnp.zeros((LEV * NY * NX,), jnp.float32).at[global_cell].add(obs_values).reshape(LEV, NY, NX)
        schur = (ens_perts.astype(jnp.float32) * spread[None]).astype(jnp.bfloat16)
        corr_back = correlate_all(schur, lat_corr, lon_corr, scale_weights)
        return jnp.einsum("ji,mjrc->mirc", vert_loc, corr_back.astype(jnp.float32), precision=lax.Precision.HIGHEST)

    first_grad = -adjoint(obs_weight * innovation)
    first_image = forward(first_grad)
    grad_square = jnp.sum(first_grad * first_grad)
    obs_square = jnp.sum(obs_weight * first_image * first_image)
    first_step = grad_square / (grad_square + obs_square)
    first_control = -first_step * first_grad
    misfit = -first_step * first_image - innovation
    gradient = first_control + adjoint(obs_weight * misfit)
    change = gradient - first_grad
    second_step = jnp.sum(first_control * change) / jnp.sum(change * change)
    new_control = first_control - second_step * gradient
    return new_control, gradient
```

```python
import jax
import jax.numpy as jnp
from jax import lax
from jax.sharding import Mesh
from jax.sharding import PartitionSpec as P

LAT = ("lat_0", "lat_1")
MEM = ("mem_0", "mem_1")
LAT_MEM = ("lat_0", "lat_1", "mem_0", "mem_1")


def gaussian_table(lengths, count, periodic):
    positions = jnp.arange(count, dtype=jnp.float32)
    distance = jnp.abs(positions[:, None] - positions[None, :])
    if periodic:
        distance = jnp.minimum(distance, count - distance)
    scaled = distance[None] / lengths[:, None, None]
    return jnp.exp(-0.5 * scaled * scaled).astype(jnp.bfloat16)


def correlate(level_field, tables):
    lat_corr, lon_corr, scale_weights = tables
    summed = jnp.zeros(level_field.shape, jnp.float32)
    for scale_index in range(lat_corr.shape[0]):
        across = jnp.einsum(
            "ab,bc->ac", lat_corr[scale_index], level_field, preferred_element_type=jnp.float32
        ).astype(jnp.bfloat16)
        summed = summed + scale_weights[scale_index] * jnp.einsum(
            "ac,cd->ad", across, lon_corr[scale_index], preferred_element_type=jnp.float32
        )
    return summed.astype(jnp.bfloat16)


def to_owner(band_field):
    got = lax.all_to_all(band_field, LAT, split_axis=0, concat_axis=0, tiled=True)
    return got.reshape(-1, got.shape[-1])


def to_bands(owned, bands):
    field = owned.reshape(bands, -1, owned.shape[-1])
    return lax.all_to_all(field, LAT, split_axis=0, concat_axis=0, tiled=True)


def split2(values):
    high = values.astype(jnp.bfloat16)
    low = (values - high.astype(jnp.float32)).astype(jnp.bfloat16)
    return high, low


def local(
    ens_perts,
    vert_loc,
    lat_lengths,
    lon_lengths,
    scale_weights,
    obs_cell,
    obs_accept,
    innovation,
    obs_precision,
):
    _, levels, band_rows, lon_count = ens_perts.shape
    bands = lax.axis_size(LAT)
    members = lax.axis_size(MEM)
    tables = (
        gaussian_table(lat_lengths, band_rows * bands, False),
        gaussian_table(lon_lengths, lon_count, True),
        scale_weights,
    )
    perts = ens_perts[0].astype(jnp.float32)
    obs_weight = obs_accept.astype(jnp.float32) * obs_precision
    line = obs_cell // lon_count
    column = obs_cell % lon_count
    at_column = (column[:, None] == jnp.arange(lon_count)[None, :]).astype(jnp.bfloat16)
    at_line = line[None, :] == jnp.arange(levels * band_rows)[:, None]

    def scattered(values):
        total = 0.0
        for part in split2(values):
            picked = jnp.where(at_line, part[None, :], jnp.bfloat16(0))
            total = total + jnp.dot(picked, at_column, preferred_element_type=jnp.float32)
        return total.reshape(levels, band_rows, lon_count)

    spread = scattered(obs_weight * innovation)
    weight_field = scattered(obs_weight)
    schur = (perts * spread).astype(jnp.bfloat16)
    owned = to_owner(schur)
    once = correlate(owned, tables)
    twice = correlate(once, tables)
    once_band = to_bands(once, bands).astype(jnp.float32)
    twice_band = to_bands(twice, bands).astype(jnp.float32)
    first_grad = -jnp.einsum("ji,jrc->irc", vert_loc, once_band, precision=lax.Precision.HIGHEST)
    both = jnp.einsum("ij,kj->ik", vert_loc, vert_loc, precision=lax.Precision.HIGHEST)
    corr = -jnp.einsum("ij,jrc->irc", both, twice_band, precision=lax.Precision.HIGHEST)
    partial = (perts * corr).astype(jnp.bfloat16)
    parts = lax.all_to_all(
        partial.reshape(members, -1, band_rows, lon_count), MEM, split_axis=0, concat_axis=0, tiled=True
    )
    own = jnp.sum(parts.astype(jnp.float32), axis=0).astype(jnp.bfloat16)
    image = lax.all_gather(own, MEM, axis=0, tiled=True).astype(jnp.float32)
    weighted = weight_field * image
    obs_local = jnp.where(lax.axis_index(MEM) == 0, jnp.sum(weighted * image), 0.0)
    schur_two = (perts * weighted).astype(jnp.bfloat16)
    back = to_bands(correlate(to_owner(schur_two), tables), bands).astype(jnp.float32)
    hess = jnp.einsum("ji,jrc->irc", vert_loc, back, precision=lax.Precision.HIGHEST)
    sums = lax.psum(
        jnp.stack(
            [
                jnp.sum(first_grad * first_grad),
                jnp.sum(first_grad * hess),
                jnp.sum(hess * hess),
                obs_local,
            ]
        ),
        LAT_MEM,
    )
    grad_square, cross, hess_square, obs_square = sums[0], sums[1], sums[2], sums[3]
    first_step = grad_square / (grad_square + obs_square)
    second_step = (grad_square + cross) / (grad_square + 2.0 * cross + hess_square)
    gradient = first_grad - first_step * (first_grad + hess)
    new_control = -first_step * first_grad - second_step * gradient
    return (new_control[None], gradient[None])


def solution(mesh):
    split = Mesh(mesh.devices.reshape(16, 4, 4, 2), ("lat_0", "lat_1", "mem_0", "mem_1"))
    placed = (P(MEM, None, LAT, None), P(), P(), P(), P(), P(LAT), P(LAT), P(LAT), P(LAT))
    return jax.shard_map(
        local,
        mesh=split,
        in_specs=placed,
        out_specs=(P(MEM, None, LAT, None), P(MEM, None, LAT, None)),
        check_vma=False,
    )
```

```python
import jax
import jax.numpy as jnp
from jax import lax
from jax.experimental import pallas as pl
from jax.experimental.pallas import tpu as pltpu
from jax.sharding import Mesh
from jax.sharding import PartitionSpec as P

LAT = ("lat_0", "lat_1")
MEM = ("mem_0", "mem_1")
MESH_ID = pl.DeviceIdType.MESH
NZ, NYC, NXC, NC = 16, 4, 4, 2
BANDS = NZ * NYC
MEMS = NXC * NC
LEV = 64
ROWS = 6
PAD = 8
NX = 768
LINES = ROWS * LEV
WIDE = LEV * PAD
SCALES = 3
OBS = 8192
CHUNK = 512
BF = jnp.bfloat16
F32 = jnp.float32

X1, UU, TT, X2, RR, RS, AG, SM, SL = range(9)


def iota(shape, dim):
    return lax.broadcasted_iota(jnp.int32, shape, dim)


def dot(a, b):
    return jnp.dot(a, b, preferred_element_type=F32)


def kernel(
    pert_ref,
    vert_ref,
    latlen_ref,
    lonlen_ref,
    sw_ref,
    cell_ref,
    accept_ref,
    innov_ref,
    prec_ref,
    f_ref,
    h_ref,
    sums_ref,
    perm,
    lat_tab,
    lon_tab,
    grad_mix,
    image_mix,
    line_ref,
    col_ref,
    field,
    weight,
    acc,
    across,
    flat,
    send_x,
    send_t,
    send_u,
    send_y,
    send_r,
    recv_x,
    recv_t,
    recv_u,
    recv_y,
    recv_r,
    part,
    part_in,
    own,
    image,
    row_mem,
    row_lat,
    sums_mem,
    sums_lat,
    send_sem,
    recv_sem,
):
    z = lax.axis_index("lat_0")
    y = lax.axis_index("lat_1")
    x = lax.axis_index("mem_0")
    c = lax.axis_index("mem_1")
    band = z * NYC + y
    mem = x * NC + c

    def lat_peer(k):
        j = k // NYC
        dz = NZ // 2 + ((j + 1) // 2) * (1 - 2 * (j % 2))
        zz = (z + dz) % NZ
        yy = (y + (NYC - 1) - k % NYC) % NYC
        return zz * NYC + yy, {"lat_0": zz, "lat_1": yy}

    def mem_peer(k):
        other = (mem + k) % MEMS
        return other, {"mem_0": other // NC, "mem_1": other % NC}

    barrier = pltpu.get_barrier_semaphore()

    def greet_lat(k, carry):
        pl.semaphore_signal(barrier, inc=1, device_id=lat_peer(k)[1], device_id_type=MESH_ID)
        return carry

    def greet_mem(k, carry):
        pl.semaphore_signal(barrier, inc=1, device_id=mem_peer(k)[1], device_id_type=MESH_ID)
        return carry

    lax.fori_loop(0, BANDS - 1, greet_lat, 0)
    lax.fori_loop(1, MEMS, greet_mem, 0)

    def remote(src, dst, phase, to):
        return pltpu.make_async_remote_copy(
            src_ref=src,
            dst_ref=dst,
            send_sem=send_sem.at[phase],
            recv_sem=recv_sem.at[phase],
            device_id=to,
            device_id_type=MESH_ID,
        )

    def lat_start(src, dst, phase):
        def go(k, carry):
            there, to = lat_peer(k)
            remote(src.at[there, pl.ds(0, ROWS)], dst.at[band, pl.ds(0, ROWS)], phase, to).start()
            return carry

        lax.fori_loop(0, BANDS - 1, go, 0)
        dst[band] = src[band]

    def wait_bytes(ref, sem):
        pltpu.make_async_copy(ref, ref, sem).wait()

    def lat_recv(dst, phase):
        wait_bytes(dst.at[pl.ds(0, BANDS - 1), pl.ds(0, ROWS)], recv_sem.at[phase])

    def lat_sent(src, phase):
        wait_bytes(src.at[pl.ds(0, BANDS - 1), pl.ds(0, ROWS)], send_sem.at[phase])

    def clear(buffer):
        buffer[:, ROWS:PAD, :] = jnp.zeros((BANDS, PAD - ROWS, NX), BF)

    cell = cell_ref[...]
    line = ((cell.astype(F32) + 0.5) * (1.0 / NX)).astype(jnp.int32)
    level = ((line.astype(F32) + 0.5) * (1.0 / ROWS)).astype(jnp.int32)
    col_ref[...] = cell - line * NX
    line_ref[...] = (line - level * ROWS) * LEV + level

    def scatter(target, with_innovation):
        target[...] = jnp.zeros((LINES, NX), F32)

        def step(k, carry):
            here = pl.ds(pl.multiple_of(k * CHUNK, CHUNK), CHUNK)
            values = accept_ref[:, here].astype(F32) * prec_ref[:, here]
            if with_innovation:
                values = values * innov_ref[:, here]
            high = values.astype(BF).astype(F32)
            at_line = iota((LINES, CHUNK), 0) == line_ref[:, here]
            at_col = (iota((NX, CHUNK), 0) == col_ref[:, here]).astype(F32).astype(BF)
            total = target[...]
            for piece in (high, values - high):
                picked = jnp.where(at_line, piece, 0.0).astype(BF)
                total = total + lax.dot_general(
                    picked, at_col, (((1,), (1,)), ((), ())), preferred_element_type=F32
                )
            target[...] = total
            return carry

        lax.fori_loop(0, OBS // CHUNK, step, 0)

    def spread_out(values, target):
        target[...] = dot(perm[...], values.astype(BF)).astype(BF).reshape(LEV, PAD, NX)

    def correlate(source, target):
        flat[...] = source[...].reshape(WIDE, NX)
        acc[...] = jnp.zeros((WIDE, NX), F32)

        def scale(s, carry):
            across[...] = dot(lat_tab[s], flat[...]).astype(BF)
            acc[...] += sw_ref[s] * dot(across[...], lon_tab[s])
            return carry

        lax.fori_loop(0, SCALES, scale, 0)
        target[...] = acc[...].astype(BF).reshape(LEV, PAD, NX)

    def mix(tables, source):
        flat[...] = source[...].reshape(WIDE, NX)
        return dot(tables[0], flat[...]) + dot(tables[1], flat[...])

    def build_perm():
        row, col = iota((WIDE, LINES), 0), iota((WIDE, LINES), 1)
        inner = row % PAD
        match = jnp.logical_and(inner < ROWS, inner * LEV + row // PAD == col)
        perm[...] = match.astype(F32).astype(BF)

    def build_tables():
        def lat(s, carry):
            row, col = iota((WIDE, WIDE), 0), iota((WIDE, WIDE), 1)
            valid = jnp.logical_and(row % PAD < ROWS, col % PAD < ROWS)
            gap = (row // PAD - col // PAD) * ROWS + row % PAD - col % PAD
            scaled = gap.astype(F32) / latlen_ref[s]
            lat_tab[s] = jnp.where(valid, jnp.exp(-0.5 * scaled * scaled), 0.0).astype(BF)
            return carry

        lax.fori_loop(0, SCALES, lat, 0)

        def lon(s, carry):
            gap = jnp.abs(iota((NX, NX), 0) - iota((NX, NX), 1))
            scaled = jnp.minimum(gap, NX - gap).astype(F32) / lonlen_ref[s]
            lon_tab[s] = jnp.exp(-0.5 * scaled * scaled).astype(BF)
            return carry

        lax.fori_loop(0, SCALES, lon, 0)
        vert = vert_ref[...]
        both = lax.dot_general(
            vert,
            vert,
            (((1,), (1,)), ((), ())),
            precision=lax.Precision.HIGHEST,
            preferred_element_type=F32,
        )
        pick_row = (iota((LINES, LEV), 0) % LEV == iota((LINES, LEV), 1)).astype(F32).astype(BF)
        pick_col = (iota((LEV, WIDE), 1) // PAD == iota((LEV, WIDE), 0)).astype(F32).astype(BF)
        same = iota((LINES, WIDE), 0) // LEV == iota((LINES, WIDE), 1) % PAD
        for matrix, target in ((vert.T, grad_mix), (both, image_mix)):
            high = matrix.astype(BF)
            low = (matrix - high.astype(F32)).astype(BF)
            for index, piece in enumerate((high, low)):
                rows = dot(pick_row, piece).astype(BF)
                target[index] = jnp.where(same, -dot(rows, pick_col), 0.0).astype(BF)

    def pert():
        return pert_ref[...].astype(F32).reshape(LINES, NX)

    for buffer in (recv_x, recv_t, recv_u, recv_y, recv_r):
        clear(buffer)
    build_perm()
    scatter(field, True)
    spread_out(pert() * field[...], send_x)
    pl.semaphore_wait(barrier, BANDS - 1 + MEMS - 1)
    lat_start(send_x, recv_x, X1)
    build_tables()
    scatter(weight, False)
    lat_recv(recv_x, X1)
    correlate(recv_x, send_t)
    correlate(send_t, send_u)
    lat_start(send_u, recv_u, UU)
    lat_start(send_t, recv_t, TT)
    lat_recv(recv_u, UU)

    part[...] = (pert() * mix(image_mix, recv_u)).reshape(ROWS, MEMS, LEV // MEMS, NX).astype(BF)

    def share(k, carry):
        other, to = mem_peer(k)
        remote(part.at[:, other], part_in.at[mem], RS, to).start()
        return carry

    lax.fori_loop(1, MEMS, share, 0)
    part_in[mem] = part[:, mem]
    wait_bytes(part_in.at[pl.ds(0, MEMS - 1)], recv_sem.at[RS])
    own[...] = jnp.sum(part_in[...].astype(F32), axis=0).astype(BF)

    def gather(k, carry):
        _, to = mem_peer(k)
        remote(own, image.at[:, mem], AG, to).start()
        return carry

    lax.fori_loop(1, MEMS, gather, 0)
    image[:, mem] = own[...]
    wait_bytes(image.at[:, pl.ds(0, MEMS - 1)], recv_sem.at[AG])
    field[...] = image[...].astype(F32).reshape(LINES, NX)
    spread_out(pert() * (weight[...] * field[...]), send_y)
    lat_start(send_y, recv_y, X2)
    obs_square = jnp.sum(weight[...] * field[...] * field[...])
    obs_square = jnp.where(mem == 0, obs_square, 0.0)
    lat_recv(recv_t, TT)
    f_ref[...] = mix(grad_mix, recv_t)
    grad_square = jnp.sum(f_ref[...] * f_ref[...])
    lat_recv(recv_y, X2)
    correlate(recv_y, send_r)
    lat_start(send_r, recv_r, RR)
    lat_recv(recv_r, RR)
    h_ref[...] = -mix(grad_mix, recv_r)
    cross = jnp.sum(f_ref[...] * h_ref[...])
    hess_square = jnp.sum(h_ref[...] * h_ref[...])

    lane = iota((1, 128), 1)
    row = jnp.zeros((1, 128), F32)
    for index, value in enumerate((grad_square, cross, hess_square, obs_square)):
        row = jnp.where(lane == index, value, row)
    row_mem[...] = row

    def tell_mem(k, carry):
        _, to = mem_peer(k)
        remote(row_mem, sums_mem.at[mem], SM, to).start()
        return carry

    lax.fori_loop(1, MEMS, tell_mem, 0)
    sums_mem[mem] = row
    wait_bytes(sums_mem.at[pl.ds(0, MEMS - 1)], recv_sem.at[SM])
    row = jnp.sum(sums_mem[...], axis=0)
    row_lat[...] = row

    def tell_lat(k, carry):
        _, to = lat_peer(k)
        remote(row_lat, sums_lat.at[band], SL, to).start()
        return carry

    lax.fori_loop(0, BANDS - 1, tell_lat, 0)
    sums_lat[band] = row
    wait_bytes(sums_lat.at[pl.ds(0, BANDS - 1)], recv_sem.at[SL])
    sums_ref[...] = jnp.sum(sums_lat[...], axis=0)

    for buffer, phase in ((send_x, X1), (send_u, UU), (send_t, TT), (send_y, X2), (send_r, RR)):
        lat_sent(buffer, phase)
    wait_bytes(part_in.at[pl.ds(0, MEMS - 1)], send_sem.at[RS])
    wait_bytes(image.at[:, pl.ds(0, MEMS - 1)], send_sem.at[AG])
    wait_bytes(sums_mem.at[pl.ds(0, MEMS - 1)], send_sem.at[SM])
    wait_bytes(sums_lat.at[pl.ds(0, BANDS - 1)], send_sem.at[SL])


def local(
    ens_perts,
    vert_loc,
    lat_lengths,
    lon_lengths,
    scale_weights,
    obs_cell,
    obs_accept,
    innovation,
    obs_precision,
):
    vmem = pl.BlockSpec(memory_space=pltpu.VMEM)
    smem = pl.BlockSpec(memory_space=pltpu.SMEM)
    slab = pltpu.VMEM((BANDS, PAD, NX), BF)
    lines = pltpu.VMEM((LINES, NX), F32)
    grad, hess, sums = pl.pallas_call(
        kernel,
        out_shape=(
            jax.ShapeDtypeStruct((LINES, NX), F32),
            jax.ShapeDtypeStruct((LINES, NX), F32),
            jax.ShapeDtypeStruct((1, 128), F32),
        ),
        in_specs=[vmem, vmem, smem, smem, smem, vmem, vmem, vmem, vmem],
        out_specs=(vmem, vmem, vmem),
        scratch_shapes=[
            pltpu.VMEM((WIDE, LINES), BF),
            pltpu.VMEM((SCALES, WIDE, WIDE), BF),
            pltpu.VMEM((SCALES, NX, NX), BF),
            pltpu.VMEM((2, LINES, WIDE), BF),
            pltpu.VMEM((2, LINES, WIDE), BF),
            pltpu.VMEM((1, OBS), jnp.int32),
            pltpu.VMEM((1, OBS), jnp.int32),
            lines,
            lines,
            pltpu.VMEM((WIDE, NX), F32),
            pltpu.VMEM((WIDE, NX), BF),
            pltpu.VMEM((WIDE, NX), BF),
            slab,
            slab,
            slab,
            slab,
            slab,
            slab,
            slab,
            slab,
            slab,
            slab,
            pltpu.VMEM((ROWS, MEMS, LEV // MEMS, NX), BF),
            pltpu.VMEM((MEMS, ROWS, LEV // MEMS, NX), BF),
            pltpu.VMEM((ROWS, LEV // MEMS, NX), BF),
            pltpu.VMEM((ROWS, MEMS, LEV // MEMS, NX), BF),
            pltpu.VMEM((1, 128), F32),
            pltpu.VMEM((1, 128), F32),
            pltpu.VMEM((MEMS, 1, 128), F32),
            pltpu.VMEM((BANDS, 1, 128), F32),
            pltpu.SemaphoreType.DMA((9,)),
            pltpu.SemaphoreType.DMA((9,)),
        ],
        compiler_params=pltpu.CompilerParams(
            collective_id=0, has_side_effects=True, vmem_limit_bytes=60 * 1024 * 1024
        ),
    )(
        ens_perts[0].transpose(1, 0, 2),
        vert_loc,
        lat_lengths,
        lon_lengths,
        scale_weights,
        obs_cell.reshape(1, OBS),
        obs_accept.reshape(1, OBS),
        innovation.reshape(1, OBS),
        obs_precision.reshape(1, OBS),
    )
    grad_square, cross, hess_square, obs_square = sums[0, 0], sums[0, 1], sums[0, 2], sums[0, 3]
    first_step = grad_square / (grad_square + obs_square)
    second_step = (grad_square + cross) / (grad_square + 2.0 * cross + hess_square)
    gradient = grad - first_step * (grad + hess)
    new_control = -first_step * grad - second_step * gradient

    def placed(field):
        return field.reshape(ROWS, LEV, NX).transpose(1, 0, 2)[None]

    return (placed(new_control), placed(gradient))


def solution(mesh):
    split = Mesh(mesh.devices.reshape(NZ, NYC, NXC, NC), ("lat_0", "lat_1", "mem_0", "mem_1"))
    placed = (P(MEM, None, LAT, None), P(), P(), P(), P(), P(LAT), P(LAT), P(LAT), P(LAT))
    return jax.shard_map(
        local,
        mesh=split,
        in_specs=placed,
        out_specs=(P(MEM, None, LAT, None), P(MEM, None, LAT, None)),
        check_vma=False,
    )
```

```python
import jax
import jax.numpy as jnp
from jax import lax
from jax.experimental import pallas as pl
from jax.experimental.pallas import tpu as pltpu
from jax.sharding import Mesh
from jax.sharding import PartitionSpec as P

LAT = ("lat_0", "lat_1")
MEM = ("mem_0", "mem_1")
MESH_ID = pl.DeviceIdType.MESH
NZ, NYC, NXC, NC = 16, 4, 4, 2
BANDS = NZ * NYC
MEMS = NXC * NC
LEV = 64
ROWS = 6
PAD = 8
NX = 768
LINES = ROWS * LEV
WIDE = LEV * PAD
SCALES = 3
OBS = 8192
BLOCK = 256
EDGE = 128
CHUNK = 512
BF = jnp.bfloat16
F32 = jnp.float32

X1, UU, TT, X2, RR, RS, AG, SM, SL = range(9)


def iota(shape, dim):
    return lax.broadcasted_iota(jnp.int32, shape, dim)


def dot(a, b):
    return jnp.dot(a, b, preferred_element_type=F32)


def kernel(
    pert_ref,
    vert_ref,
    latlen_ref,
    lonlen_ref,
    sw_ref,
    cell_ref,
    accept_ref,
    innov_ref,
    prec_ref,
    control_ref,
    gradient_ref,
    perm,
    lat_tab,
    lon_tab,
    grad_mix,
    image_mix,
    line_ref,
    col_ref,
    field,
    weight,
    acc,
    across,
    flat,
    send_x,
    send_t,
    send_u,
    send_y,
    send_r,
    recv_x,
    recv_t,
    recv_u,
    recv_y,
    recv_r,
    part,
    part_in,
    own,
    image,
    f_ref,
    h_ref,
    row_mem,
    row_lat,
    sums_mem,
    sums_lat,
    send_sem,
    recv_sem,
):
    z = lax.axis_index("lat_0")
    y = lax.axis_index("lat_1")
    x = lax.axis_index("mem_0")
    c = lax.axis_index("mem_1")
    band = z * NYC + y
    mem = x * NC + c

    def lat_peer(k):
        j = k // NYC
        dz = NZ // 2 + ((j + 1) // 2) * (1 - 2 * (j % 2))
        zz = (z + dz) % NZ
        yy = (y + (NYC - 1) - k % NYC) % NYC
        return zz * NYC + yy, {"lat_0": zz, "lat_1": yy}

    def mem_peer(k):
        other = (mem + k) % MEMS
        return other, {"mem_0": other // NC, "mem_1": other % NC}

    barrier = pltpu.get_barrier_semaphore()

    def greet_lat(k, carry):
        pl.semaphore_signal(barrier, inc=1, device_id=lat_peer(k)[1], device_id_type=MESH_ID)
        return carry

    def greet_mem(k, carry):
        pl.semaphore_signal(barrier, inc=1, device_id=mem_peer(k)[1], device_id_type=MESH_ID)
        return carry

    lax.fori_loop(0, BANDS - 1, greet_lat, 0)
    lax.fori_loop(1, MEMS, greet_mem, 0)

    def remote(src, dst, phase, to):
        return pltpu.make_async_remote_copy(
            src_ref=src,
            dst_ref=dst,
            send_sem=send_sem.at[phase],
            recv_sem=recv_sem.at[phase],
            device_id=to,
            device_id_type=MESH_ID,
        )

    def lat_start(src, dst, phase):
        def go(k, carry):
            there, to = lat_peer(k)
            remote(src.at[there, pl.ds(0, ROWS)], dst.at[band, pl.ds(0, ROWS)], phase, to).start()
            return carry

        lax.fori_loop(0, BANDS - 1, go, 0)
        dst[band] = src[band]

    def wait_bytes(ref, sem):
        pltpu.make_async_copy(ref, ref, sem).wait()

    def lat_recv(dst, phase):
        wait_bytes(dst.at[pl.ds(0, BANDS - 1), pl.ds(0, ROWS)], recv_sem.at[phase])

    def lat_sent(src, phase):
        wait_bytes(src.at[pl.ds(0, BANDS - 1), pl.ds(0, ROWS)], send_sem.at[phase])

    def clear(buffer):
        buffer[:, ROWS:PAD, :] = jnp.zeros((BANDS, PAD - ROWS, NX), BF)

    cell = cell_ref[...]
    line = ((cell.astype(F32) + 0.5) * (1.0 / NX)).astype(jnp.int32)
    level = ((line.astype(F32) + 0.5) * (1.0 / ROWS)).astype(jnp.int32)
    col_ref[...] = cell - line * NX
    line_ref[...] = (line - level * ROWS) * LEV + level

    def scatter(target, with_innovation):
        target[...] = jnp.zeros((LINES, NX), F32)

        def step(k, carry):
            here = pl.ds(pl.multiple_of(k * CHUNK, CHUNK), CHUNK)
            values = accept_ref[:, here].astype(F32) * prec_ref[:, here]
            if with_innovation:
                values = values * innov_ref[:, here]
            high = values.astype(BF).astype(F32)
            at_line = iota((LINES, CHUNK), 0) == line_ref[:, here]
            at_col = (iota((NX, CHUNK), 0) == col_ref[:, here]).astype(F32).astype(BF)
            total = target[...]
            for piece in (high,) if with_innovation else (high, values - high):
                picked = jnp.where(at_line, piece, 0.0).astype(BF)
                total = total + lax.dot_general(
                    picked, at_col, (((1,), (1,)), ((), ())), preferred_element_type=F32
                )
            target[...] = total
            return carry

        lax.fori_loop(0, OBS // CHUNK, step, 0)

    def spread_out(values, target):
        target[...] = dot(perm[...], values.astype(BF)).astype(BF).reshape(LEV, PAD, NX)

    def correlate(source, target):
        flat[...] = source[...].reshape(WIDE, NX)
        acc[...] = jnp.zeros((WIDE, NX), F32)

        def scale(s, carry):
            rows = dot(lat_tab[s], flat[...]).astype(BF)
            across[:, EDGE : EDGE + NX] = rows
            across[:, :EDGE] = rows[:, NX - EDGE :]
            across[:, EDGE + NX :] = rows[:, :EDGE]
            for first in range(0, NX, BLOCK):
                window = across[:, first : first + BLOCK + 2 * EDGE]
                acc[:, first : first + BLOCK] += sw_ref[s] * dot(window, lon_tab[s])
            return carry

        lax.fori_loop(0, SCALES, scale, 0)
        target[...] = acc[...].astype(BF).reshape(LEV, PAD, NX)

    def mix(tables, source):
        flat[...] = source[...].reshape(WIDE, NX)
        return dot(tables[0], flat[...]) + dot(tables[1], flat[...])

    def build_perm():
        row, col = iota((WIDE, LINES), 0), iota((WIDE, LINES), 1)
        inner = row % PAD
        match = jnp.logical_and(inner < ROWS, inner * LEV + row // PAD == col)
        perm[...] = match.astype(F32).astype(BF)

    def build_tables():
        def lat(s, carry):
            row, col = iota((WIDE, WIDE), 0), iota((WIDE, WIDE), 1)
            valid = jnp.logical_and(row % PAD < ROWS, col % PAD < ROWS)
            gap = (row // PAD - col // PAD) * ROWS + row % PAD - col % PAD
            scaled = gap.astype(F32) / latlen_ref[s]
            lat_tab[s] = jnp.where(valid, jnp.exp(-0.5 * scaled * scaled), 0.0).astype(BF)
            return carry

        lax.fori_loop(0, SCALES, lat, 0)

        def lon(s, carry):
            tall = (BLOCK + 2 * EDGE, BLOCK)
            gap = iota(tall, 0) - EDGE - iota(tall, 1)
            scaled = gap.astype(F32) / lonlen_ref[s]
            lon_tab[s] = jnp.exp(-0.5 * scaled * scaled).astype(BF)
            return carry

        lax.fori_loop(0, SCALES, lon, 0)
        vert = vert_ref[...]
        both = lax.dot_general(
            vert,
            vert,
            (((1,), (1,)), ((), ())),
            precision=lax.Precision.HIGHEST,
            preferred_element_type=F32,
        )
        pick_row = (iota((LINES, LEV), 0) % LEV == iota((LINES, LEV), 1)).astype(F32).astype(BF)
        pick_col = (iota((LEV, WIDE), 1) // PAD == iota((LEV, WIDE), 0)).astype(F32).astype(BF)
        same = iota((LINES, WIDE), 0) // LEV == iota((LINES, WIDE), 1) % PAD
        for matrix, target in ((vert.T, grad_mix), (both, image_mix)):
            high = matrix.astype(BF)
            low = (matrix - high.astype(F32)).astype(BF)
            for index, piece in enumerate((high, low)):
                rows = dot(pick_row, piece).astype(BF)
                target[index] = jnp.where(same, -dot(rows, pick_col), 0.0).astype(BF)

    def pert():
        return pert_ref[...].astype(F32).reshape(LINES, NX)

    for buffer in (recv_x, recv_t, recv_u, recv_y, recv_r):
        clear(buffer)
    build_perm()
    scatter(field, True)
    spread_out(pert() * field[...], send_x)
    pl.semaphore_wait(barrier, BANDS - 1 + MEMS - 1)
    lat_start(send_x, recv_x, X1)
    build_tables()
    lat_recv(recv_x, X1)
    correlate(recv_x, send_t)
    correlate(send_t, send_u)
    lat_start(send_u, recv_u, UU)
    lat_start(send_t, recv_t, TT)
    scatter(weight, False)
    lat_recv(recv_u, UU)

    part[...] = (pert() * mix(image_mix, recv_u)).reshape(ROWS, MEMS, LEV // MEMS, NX).astype(BF)

    def share(k, carry):
        other, to = mem_peer(k)
        remote(part.at[:, other], part_in.at[mem], RS, to).start()
        return carry

    lax.fori_loop(1, MEMS, share, 0)
    part_in[mem] = part[:, mem]
    wait_bytes(part_in.at[pl.ds(0, MEMS - 1)], recv_sem.at[RS])
    own[...] = jnp.sum(part_in[...].astype(F32), axis=0).astype(BF)

    def gather(k, carry):
        _, to = mem_peer(k)
        remote(own, image.at[:, mem], AG, to).start()
        return carry

    lax.fori_loop(1, MEMS, gather, 0)
    image[:, mem] = own[...]
    wait_bytes(image.at[:, pl.ds(0, MEMS - 1)], recv_sem.at[AG])
    field[...] = image[...].astype(F32).reshape(LINES, NX)
    spread_out(pert() * (weight[...] * field[...]), send_y)
    lat_start(send_y, recv_y, X2)
    obs_square = jnp.sum(weight[...] * field[...] * field[...])
    obs_square = jnp.where(mem == 0, obs_square, 0.0)
    lat_recv(recv_t, TT)
    f_ref[...] = mix(grad_mix, recv_t)
    grad_square = jnp.sum(f_ref[...] * f_ref[...])
    lat_recv(recv_y, X2)
    correlate(recv_y, send_r)
    lat_start(send_r, recv_r, RR)
    lat_recv(recv_r, RR)
    h_ref[...] = -mix(grad_mix, recv_r)
    cross = jnp.sum(f_ref[...] * h_ref[...])
    hess_square = jnp.sum(h_ref[...] * h_ref[...])

    lane = iota((1, 128), 1)
    row = jnp.zeros((1, 128), F32)
    for index, value in enumerate((grad_square, cross, hess_square, obs_square)):
        row = jnp.where(lane == index, value, row)
    row_mem[...] = row

    def tell_mem(k, carry):
        _, to = mem_peer(k)
        remote(row_mem, sums_mem.at[mem], SM, to).start()
        return carry

    lax.fori_loop(1, MEMS, tell_mem, 0)
    sums_mem[mem] = row
    wait_bytes(sums_mem.at[pl.ds(0, MEMS - 1)], recv_sem.at[SM])
    row = jnp.sum(sums_mem[...], axis=0)
    row_lat[...] = row

    def tell_lat(k, carry):
        _, to = lat_peer(k)
        remote(row_lat, sums_lat.at[band], SL, to).start()
        return carry

    lax.fori_loop(0, BANDS - 1, tell_lat, 0)
    sums_lat[band] = row
    wait_bytes(sums_lat.at[pl.ds(0, BANDS - 1)], recv_sem.at[SL])
    total = jnp.sum(sums_lat[...], axis=0)
    grad_square, cross, hess_square, obs_square = (
        jnp.sum(jnp.where(lane == index, total, 0.0)) for index in range(4)
    )
    first_step = grad_square / (grad_square + obs_square)
    second_step = (grad_square + cross) / (grad_square + 2.0 * cross + hess_square)
    gradient = f_ref[...] - first_step * (f_ref[...] + h_ref[...])
    gradient_ref[...] = gradient
    control_ref[...] = -first_step * f_ref[...] - second_step * gradient

    for buffer, phase in ((send_x, X1), (send_u, UU), (send_t, TT), (send_y, X2), (send_r, RR)):
        lat_sent(buffer, phase)
    wait_bytes(part_in.at[pl.ds(0, MEMS - 1)], send_sem.at[RS])
    wait_bytes(image.at[:, pl.ds(0, MEMS - 1)], send_sem.at[AG])
    wait_bytes(sums_mem.at[pl.ds(0, MEMS - 1)], send_sem.at[SM])
    wait_bytes(sums_lat.at[pl.ds(0, BANDS - 1)], send_sem.at[SL])


def local(
    ens_perts,
    vert_loc,
    lat_lengths,
    lon_lengths,
    scale_weights,
    obs_cell,
    obs_accept,
    innovation,
    obs_precision,
):
    vmem = pl.BlockSpec(memory_space=pltpu.VMEM)
    smem = pl.BlockSpec(memory_space=pltpu.SMEM)
    slab = pltpu.VMEM((BANDS, PAD, NX), BF)
    lines = pltpu.VMEM((LINES, NX), F32)
    new_control, gradient = pl.pallas_call(
        kernel,
        out_shape=(
            jax.ShapeDtypeStruct((LINES, NX), F32),
            jax.ShapeDtypeStruct((LINES, NX), F32),
        ),
        in_specs=[vmem, vmem, smem, smem, smem, vmem, vmem, vmem, vmem],
        out_specs=(vmem, vmem),
        scratch_shapes=[
            pltpu.VMEM((WIDE, LINES), BF),
            pltpu.VMEM((SCALES, WIDE, WIDE), BF),
            pltpu.VMEM((SCALES, BLOCK + 2 * EDGE, BLOCK), BF),
            pltpu.VMEM((2, LINES, WIDE), BF),
            pltpu.VMEM((2, LINES, WIDE), BF),
            pltpu.VMEM((1, OBS), jnp.int32),
            pltpu.VMEM((1, OBS), jnp.int32),
            lines,
            lines,
            pltpu.VMEM((WIDE, NX), F32),
            pltpu.VMEM((WIDE, NX + 2 * EDGE), BF),
            pltpu.VMEM((WIDE, NX), BF),
            slab,
            slab,
            slab,
            slab,
            slab,
            slab,
            slab,
            slab,
            slab,
            slab,
            pltpu.VMEM((ROWS, MEMS, LEV // MEMS, NX), BF),
            pltpu.VMEM((MEMS, ROWS, LEV // MEMS, NX), BF),
            pltpu.VMEM((ROWS, LEV // MEMS, NX), BF),
            pltpu.VMEM((ROWS, MEMS, LEV // MEMS, NX), BF),
            lines,
            lines,
            pltpu.VMEM((1, 128), F32),
            pltpu.VMEM((1, 128), F32),
            pltpu.VMEM((MEMS, 1, 128), F32),
            pltpu.VMEM((BANDS, 1, 128), F32),
            pltpu.SemaphoreType.DMA((9,)),
            pltpu.SemaphoreType.DMA((9,)),
        ],
        compiler_params=pltpu.CompilerParams(
            collective_id=0, has_side_effects=True, vmem_limit_bytes=40 * 1024 * 1024
        ),
    )(
        ens_perts[0].transpose(1, 0, 2),
        vert_loc,
        lat_lengths,
        lon_lengths,
        scale_weights,
        obs_cell.reshape(1, OBS),
        obs_accept.reshape(1, OBS),
        innovation.reshape(1, OBS),
        obs_precision.reshape(1, OBS),
    )

    def placed(field):
        return field.reshape(ROWS, LEV, NX).transpose(1, 0, 2)[None]

    return (placed(new_control), placed(gradient))


def solution(mesh):
    split = Mesh(mesh.devices.reshape(NZ, NYC, NXC, NC), ("lat_0", "lat_1", "mem_0", "mem_1"))
    placed = (P(MEM, None, LAT, None), P(), P(), P(), P(), P(LAT), P(LAT), P(LAT), P(LAT))
    return jax.shard_map(
        local,
        mesh=split,
        in_specs=placed,
        out_specs=(P(MEM, None, LAT, None), P(MEM, None, LAT, None)),
        check_vma=False,
    )
```

```python
import jax
import jax.numpy as jnp
from jax import lax
from jax.experimental import pallas as pl
from jax.experimental.pallas import tpu as pltpu
from jax.sharding import Mesh
from jax.sharding import PartitionSpec as P

LAT = ("lat_0", "lat_1")
MEM = ("mem_0", "mem_1")
MESH_ID = pl.DeviceIdType.MESH
NZ, NYC, NXC, NC = 16, 4, 4, 2
BANDS = NZ * NYC
MEMS = NXC * NC
LEV = 64
ROWS = 6
PAD = 8
NX = 768
LINES = ROWS * LEV
WIDE = LEV * PAD
SCALES = 3
OBS = 8192
BLOCK = 256
EDGE = 128
TILE = 128
TILES = NX // TILE
NEAR = 20
CHUNK = 512
BF = jnp.bfloat16
F32 = jnp.float32

PP, S1, A1, UU, TT, RS, S2, A2, RR, SM, SL = range(11)


def iota(shape, dim):
    return lax.broadcasted_iota(jnp.int32, shape, dim)


def dot(a, b):
    return jnp.dot(a, b, preferred_element_type=F32)


def kernel(
    pert_ref,
    vert_ref,
    latlen_ref,
    lonlen_ref,
    sw_ref,
    cell_ref,
    accept_ref,
    innov_ref,
    prec_ref,
    control_ref,
    gradient_ref,
    perm,
    lat_tab,
    lon_tab,
    grad_mix,
    image_mix,
    line_ref,
    col_ref,
    spread,
    weight,
    acc,
    across,
    flat,
    send_p,
    send_t,
    send_u,
    send_r,
    recv_p,
    recv_t,
    recv_u,
    recv_r,
    tile_out,
    tile_in,
    tiles,
    tile_out_two,
    tile_in_two,
    tiles_two,
    part,
    part_in,
    f_ref,
    h_ref,
    row_mem,
    row_lat,
    sums_mem,
    sums_lat,
    send_sem,
    recv_sem,
):
    z = lax.axis_index("lat_0")
    y = lax.axis_index("lat_1")
    x = lax.axis_index("mem_0")
    c = lax.axis_index("mem_1")
    band = z * NYC + y
    mem = x * NC + c

    def lat_peer(k):
        j = k // NYC
        dz = NZ // 2 + ((j + 1) // 2) * (1 - 2 * (j % 2))
        zz = (z + dz) % NZ
        yy = (y + (NYC - 1) - k % NYC) % NYC
        return zz * NYC + yy, {"lat_0": zz, "lat_1": yy}

    def mem_peer(k):
        other = (mem + k) % MEMS
        return other, {"mem_0": other // NC, "mem_1": other % NC}

    barrier = pltpu.get_barrier_semaphore()

    def greet_lat(k, carry):
        pl.semaphore_signal(barrier, inc=1, device_id=lat_peer(k)[1], device_id_type=MESH_ID)
        return carry

    def greet_mem(k, carry):
        pl.semaphore_signal(barrier, inc=1, device_id=mem_peer(k)[1], device_id_type=MESH_ID)
        return carry

    lax.fori_loop(0, BANDS - 1, greet_lat, 0)
    lax.fori_loop(1, MEMS, greet_mem, 0)

    def remote(src, dst, phase, to):
        return pltpu.make_async_remote_copy(
            src_ref=src,
            dst_ref=dst,
            send_sem=send_sem.at[phase],
            recv_sem=recv_sem.at[phase],
            device_id=to,
            device_id_type=MESH_ID,
        )

    def lat_start(src, dst, phase, first=0, last=BANDS - 1):
        def go(k, carry):
            there, to = lat_peer(k)
            remote(src.at[there, pl.ds(0, ROWS)], dst.at[band, pl.ds(0, ROWS)], phase, to).start()
            return carry

        lax.fori_loop(first, last, go, 0)

    def wait_bytes(ref, sem):
        pltpu.make_async_copy(ref, ref, sem).wait()

    def lat_recv(dst, phase):
        wait_bytes(dst.at[pl.ds(0, BANDS - 1), pl.ds(0, ROWS)], recv_sem.at[phase])

    def lat_sent(src, phase):
        wait_bytes(src.at[pl.ds(0, BANDS - 1), pl.ds(0, ROWS)], send_sem.at[phase])

    def clear(buffer):
        shape = (BANDS, PAD - ROWS, buffer.shape[-1])
        buffer[:, ROWS:PAD, :] = jnp.zeros(shape, BF)

    cell = cell_ref[...]
    line = ((cell.astype(F32) + 0.5) * (1.0 / NX)).astype(jnp.int32)
    level = ((line.astype(F32) + 0.5) * (1.0 / ROWS)).astype(jnp.int32)
    col_ref[...] = cell - line * NX - mem * TILE
    line_ref[...] = (line - level * ROWS) * LEV + level

    def scatter(target, with_innovation):
        target[...] = jnp.zeros((LINES, TILE), F32)

        def step(k, carry):
            here = pl.ds(pl.multiple_of(k * CHUNK, CHUNK), CHUNK)
            values = accept_ref[:, here].astype(F32) * prec_ref[:, here]
            if with_innovation:
                values = values * innov_ref[:, here]
            high = values.astype(BF).astype(F32)
            at_line = iota((LINES, CHUNK), 0) == line_ref[:, here]
            at_col = (iota((TILE, CHUNK), 0) == col_ref[:, here]).astype(F32).astype(BF)
            total = target[...]
            for piece in (high, values - high):
                picked = jnp.where(at_line, piece, 0.0).astype(BF)
                total = total + lax.dot_general(
                    picked, at_col, (((1,), (1,)), ((), ())), preferred_element_type=F32
                )
            target[...] = total
            return carry

        lax.fori_loop(0, OBS // CHUNK, step, 0)

    def by_level(values):
        return dot(perm[...], values).astype(BF).reshape(LEV, PAD, values.shape[-1])

    def tile_gather(out, inward, every, phase_lat, phase_mem):
        @pl.when(mem < TILES)
        def _():
            lat_recv(inward, phase_lat)
            inward[band] = out[band]

            def go(k, carry):
                _, to = mem_peer(k)
                remote(
                    inward.at[:, pl.ds(0, ROWS)], every.at[mem, :, pl.ds(0, ROWS)], phase_mem, to
                ).start()
                return carry

            lax.fori_loop(1, MEMS, go, 0)
            every[mem] = inward[...]
            wait_bytes(every.at[pl.ds(0, TILES - 1), :, pl.ds(0, ROWS)], recv_sem.at[phase_mem])

        @pl.when(mem >= TILES)
        def _():
            wait_bytes(every.at[pl.ds(0, TILES), :, pl.ds(0, ROWS)], recv_sem.at[phase_mem])

    def owner_schur(every):
        for t in range(TILES):
            cols = slice(t * TILE, (t + 1) * TILE)
            product = recv_p[:, :, cols].astype(F32) * every[t].astype(F32)
            flat[:, cols] = product.astype(BF).reshape(WIDE, TILE)

    def correlate(target):
        acc[...] = jnp.zeros((WIDE, NX), F32)

        def scale(s, carry):
            rows = dot(lat_tab[s], flat[...]).astype(BF)
            across[:, EDGE : EDGE + NX] = rows
            across[:, :EDGE] = rows[:, NX - EDGE :]
            across[:, EDGE + NX :] = rows[:, :EDGE]
            for first in range(0, NX, BLOCK):
                window = across[:, first : first + BLOCK + 2 * EDGE]
                acc[:, first : first + BLOCK] += sw_ref[s] * dot(window, lon_tab[s])
            return carry

        lax.fori_loop(0, SCALES, scale, 0)
        target[...] = acc[...].astype(BF).reshape(LEV, PAD, NX)

    def mix(tables, source):
        flat[...] = source[...].reshape(WIDE, NX)
        return dot(tables[0], flat[...]) + dot(tables[1], flat[...])

    def build_perm():
        row, col = iota((WIDE, LINES), 0), iota((WIDE, LINES), 1)
        inner = row % PAD
        match = jnp.logical_and(inner < ROWS, inner * LEV + row // PAD == col)
        perm[...] = match.astype(F32).astype(BF)

    def build_tables():
        def lat(s, carry):
            row, col = iota((WIDE, WIDE), 0), iota((WIDE, WIDE), 1)
            valid = jnp.logical_and(row % PAD < ROWS, col % PAD < ROWS)
            gap = (row // PAD - col // PAD) * ROWS + row % PAD - col % PAD
            scaled = gap.astype(F32) / latlen_ref[s]
            lat_tab[s] = jnp.where(valid, jnp.exp(-0.5 * scaled * scaled), 0.0).astype(BF)
            return carry

        lax.fori_loop(0, SCALES, lat, 0)

        def lon(s, carry):
            tall = (BLOCK + 2 * EDGE, BLOCK)
            gap = iota(tall, 0) - EDGE - iota(tall, 1)
            scaled = gap.astype(F32) / lonlen_ref[s]
            lon_tab[s] = jnp.exp(-0.5 * scaled * scaled).astype(BF)
            return carry

        lax.fori_loop(0, SCALES, lon, 0)
        vert = vert_ref[...]
        both = lax.dot_general(
            vert,
            vert,
            (((1,), (1,)), ((), ())),
            precision=lax.Precision.HIGHEST,
            preferred_element_type=F32,
        )
        pick_row = (iota((LINES, LEV), 0) % LEV == iota((LINES, LEV), 1)).astype(F32).astype(BF)
        pick_col = (iota((LEV, WIDE), 1) // PAD == iota((LEV, WIDE), 0)).astype(F32).astype(BF)
        same = iota((LINES, WIDE), 0) // LEV == iota((LINES, WIDE), 1) % PAD
        for matrix, target in ((vert.T, grad_mix), (both, image_mix)):
            high = matrix.astype(BF)
            low = (matrix - high.astype(F32)).astype(BF)
            for index, piece in enumerate((high, low)):
                rows = dot(pick_row, piece).astype(BF)
                target[index] = jnp.where(same, -dot(rows, pick_col), 0.0).astype(BF)

    def pert():
        return pert_ref[...].astype(F32).reshape(LINES, NX)

    for buffer in (recv_p, recv_t, recv_u, recv_r):
        clear(buffer)
    for buffer in (tile_in, tile_in_two):
        clear(buffer)
    for every in (tiles, tiles_two):
        for t in range(TILES):
            clear(every.at[t])
    build_perm()
    scatter(spread, True)
    tile_out[...] = by_level(spread[...].astype(BF))
    pl.semaphore_wait(barrier, BANDS - 1 + MEMS - 1)

    @pl.when(mem < TILES)
    def _():
        lat_start(tile_out, tile_in, S1)

    send_p[...] = by_level(pert_ref[...].reshape(LINES, NX))
    lat_start(send_p, recv_p, PP)
    build_tables()
    tile_gather(tile_out, tile_in, tiles, S1, A1)
    scatter(weight, False)
    recv_p[band] = send_p[band]
    lat_recv(recv_p, PP)
    owner_schur(tiles)
    correlate(send_t)
    flat[...] = send_t[...].reshape(WIDE, NX)
    correlate(send_u)
    lat_start(send_u, recv_u, UU)
    lat_start(send_t, recv_t, TT, 0, NEAR)
    recv_u[band] = send_u[band]
    recv_t[band] = send_t[band]
    lat_recv(recv_u, UU)

    partial = (pert() * mix(image_mix, recv_u)).astype(BF)
    for t in range(TILES):
        part[t] = partial[:, t * TILE : (t + 1) * TILE]

    def share(k, carry):
        there = (mem + k) % TILES

        @pl.when(there != mem)
        def _():
            to = {"mem_0": there // NC, "mem_1": there % NC}
            remote(part.at[there], part_in.at[mem], RS, to).start()

        return carry

    lax.fori_loop(0, TILES, share, 0)

    @pl.when(mem < TILES)
    def _():
        part_in[mem] = part[mem]
        wait_bytes(part_in.at[pl.ds(0, MEMS - 1)], recv_sem.at[RS])
        image = jnp.sum(part_in[...].astype(F32), axis=0)
        weighted = weight[...] * image
        spread[...] = weighted * image
        tile_out_two[...] = by_level(weighted.astype(BF))
        lat_start(tile_out_two, tile_in_two, S2)

    @pl.when(mem >= TILES)
    def _():
        spread[...] = jnp.zeros((LINES, TILE), F32)

    lat_start(send_t, recv_t, TT, NEAR, BANDS - 1)
    obs_square = jnp.sum(spread[...])
    tile_gather(tile_out_two, tile_in_two, tiles_two, S2, A2)
    owner_schur(tiles_two)
    correlate(send_r)
    lat_start(send_r, recv_r, RR)
    recv_r[band] = send_r[band]
    lat_recv(recv_t, TT)
    f_ref[...] = mix(grad_mix, recv_t)
    grad_square = jnp.sum(f_ref[...] * f_ref[...])
    lat_recv(recv_r, RR)
    h_ref[...] = -mix(grad_mix, recv_r)
    cross = jnp.sum(f_ref[...] * h_ref[...])
    hess_square = jnp.sum(h_ref[...] * h_ref[...])

    lane = iota((1, 128), 1)
    row = jnp.zeros((1, 128), F32)
    for index, value in enumerate((grad_square, cross, hess_square, obs_square)):
        row = jnp.where(lane == index, value, row)
    row_mem[...] = row

    def tell_mem(k, carry):
        _, to = mem_peer(k)
        remote(row_mem, sums_mem.at[mem], SM, to).start()
        return carry

    lax.fori_loop(1, MEMS, tell_mem, 0)
    sums_mem[mem] = row
    wait_bytes(sums_mem.at[pl.ds(0, MEMS - 1)], recv_sem.at[SM])
    row = jnp.sum(sums_mem[...], axis=0)
    row_lat[...] = row

    def tell_lat(k, carry):
        _, to = lat_peer(k)
        remote(row_lat, sums_lat.at[band], SL, to).start()
        return carry

    lax.fori_loop(0, BANDS - 1, tell_lat, 0)
    sums_lat[band] = row
    wait_bytes(sums_lat.at[pl.ds(0, BANDS - 1)], recv_sem.at[SL])
    total = jnp.sum(sums_lat[...], axis=0)
    grad_square, cross, hess_square, obs_square = (
        jnp.sum(jnp.where(lane == index, total, 0.0)) for index in range(4)
    )
    first_step = grad_square / (grad_square + obs_square)
    second_step = (grad_square + cross) / (grad_square + 2.0 * cross + hess_square)
    gradient = f_ref[...] - first_step * (f_ref[...] + h_ref[...])
    gradient_ref[...] = gradient
    control_ref[...] = -first_step * f_ref[...] - second_step * gradient

    for buffer, phase in ((send_p, PP), (send_u, UU), (send_t, TT), (send_r, RR)):
        lat_sent(buffer, phase)

    @pl.when(mem < TILES)
    def _():
        lat_sent(tile_out, S1)
        lat_sent(tile_out_two, S2)
        for every, phase in ((tiles, A1), (tiles_two, A2)):
            wait_bytes(every.at[pl.ds(0, MEMS - 1), :, pl.ds(0, ROWS)], send_sem.at[phase])
        wait_bytes(part_in.at[pl.ds(0, TILES - 1)], send_sem.at[RS])

    @pl.when(mem >= TILES)
    def _():
        wait_bytes(part_in.at[pl.ds(0, TILES)], send_sem.at[RS])

    wait_bytes(sums_mem.at[pl.ds(0, MEMS - 1)], send_sem.at[SM])
    wait_bytes(sums_lat.at[pl.ds(0, BANDS - 1)], send_sem.at[SL])


def local(
    ens_perts,
    vert_loc,
    lat_lengths,
    lon_lengths,
    scale_weights,
    obs_cell,
    obs_accept,
    innovation,
    obs_precision,
):
    vmem = pl.BlockSpec(memory_space=pltpu.VMEM)
    smem = pl.BlockSpec(memory_space=pltpu.SMEM)
    slab = pltpu.VMEM((BANDS, PAD, NX), BF)
    lines = pltpu.VMEM((LINES, NX), F32)
    chunk = pltpu.VMEM((LINES, TILE), F32)
    level_tile = pltpu.VMEM((BANDS, PAD, TILE), BF)
    all_tiles = pltpu.VMEM((MEMS, BANDS, PAD, TILE), BF)
    new_control, gradient = pl.pallas_call(
        kernel,
        out_shape=(
            jax.ShapeDtypeStruct((LINES, NX), F32),
            jax.ShapeDtypeStruct((LINES, NX), F32),
        ),
        in_specs=[vmem, vmem, smem, smem, smem, vmem, vmem, vmem, vmem],
        out_specs=(vmem, vmem),
        scratch_shapes=[
            pltpu.VMEM((WIDE, LINES), BF),
            pltpu.VMEM((SCALES, WIDE, WIDE), BF),
            pltpu.VMEM((SCALES, BLOCK + 2 * EDGE, BLOCK), BF),
            pltpu.VMEM((2, LINES, WIDE), BF),
            pltpu.VMEM((2, LINES, WIDE), BF),
            pltpu.VMEM((1, OBS), jnp.int32),
            pltpu.VMEM((1, OBS), jnp.int32),
            chunk,
            chunk,
            pltpu.VMEM((WIDE, NX), F32),
            pltpu.VMEM((WIDE, NX + 2 * EDGE), BF),
            pltpu.VMEM((WIDE, NX), BF),
            slab,
            slab,
            slab,
            slab,
            slab,
            slab,
            slab,
            slab,
            level_tile,
            level_tile,
            all_tiles,
            level_tile,
            level_tile,
            all_tiles,
            pltpu.VMEM((TILES, LINES, TILE), BF),
            pltpu.VMEM((MEMS, LINES, TILE), BF),
            lines,
            lines,
            pltpu.VMEM((1, 128), F32),
            pltpu.VMEM((1, 128), F32),
            pltpu.VMEM((MEMS, 1, 128), F32),
            pltpu.VMEM((BANDS, 1, 128), F32),
            pltpu.SemaphoreType.DMA((11,)),
            pltpu.SemaphoreType.DMA((11,)),
        ],
        compiler_params=pltpu.CompilerParams(
            collective_id=0, has_side_effects=True, vmem_limit_bytes=62 * 1024 * 1024
        ),
    )(
        ens_perts[0].transpose(1, 0, 2),
        vert_loc,
        lat_lengths,
        lon_lengths,
        scale_weights,
        obs_cell.reshape(1, OBS),
        obs_accept.reshape(1, OBS),
        innovation.reshape(1, OBS),
        obs_precision.reshape(1, OBS),
    )

    def placed(field):
        return field.reshape(ROWS, LEV, NX).transpose(1, 0, 2)[None]

    return (placed(new_control), placed(gradient))


def solution(mesh):
    split = Mesh(mesh.devices.reshape(NZ, NYC, NXC, NC), ("lat_0", "lat_1", "mem_0", "mem_1"))
    placed = (P(MEM, None, LAT, None), P(), P(), P(), P(), P(LAT), P(LAT), P(LAT), P(LAT))
    return jax.shard_map(
        local,
        mesh=split,
        in_specs=placed,
        out_specs=(P(MEM, None, LAT, None), P(MEM, None, LAT, None)),
        check_vma=False,
    )
```

```python
import jax
import jax.numpy as jnp
from jax import lax
from jax.experimental import pallas as pl
from jax.experimental.pallas import tpu as pltpu
from jax.sharding import Mesh
from jax.sharding import PartitionSpec as P

LAT = ("lat_0", "lat_1")
MEM = ("mem_0", "mem_1")
MESH_ID = pl.DeviceIdType.MESH
NZ, NYC, NXC, NC = 16, 4, 4, 2
BANDS = NZ * NYC
MEMS = NXC * NC
LEV = 64
ROWS = 6
PAD = 8
NX = 768
LINES = ROWS * LEV
WIDE = LEV * PAD
SCALES = 3
OBS = 8192
BLOCK = 256
EDGE = 128
TILE = 128
TILES = NX // TILE
GROUP = 256
GROUPS = NX // GROUP
EARLY = 4
NEAR = 8
CHUNK = 512
BF = jnp.bfloat16
F32 = jnp.float32

PP, S1, A1, TT, RS, S2, A2, RR, SM, SL, UU = range(11)


def iota(shape, dim):
    return lax.broadcasted_iota(jnp.int32, shape, dim)


def dot(a, b):
    return jnp.dot(a, b, preferred_element_type=F32)


def kernel(
    pert_ref,
    vert_ref,
    latlen_ref,
    lonlen_ref,
    sw_ref,
    cell_ref,
    accept_ref,
    innov_ref,
    prec_ref,
    control_ref,
    gradient_ref,
    perm,
    lat_tab,
    lon_tab,
    grad_mix,
    image_mix,
    line_ref,
    col_ref,
    spread,
    weight,
    acc,
    across,
    flat,
    send_p,
    send_t,
    send_u,
    send_r,
    recv_p,
    recv_t,
    recv_u,
    recv_r,
    tile_out,
    tile_in,
    tiles,
    tile_out_two,
    tile_in_two,
    tiles_two,
    part,
    part_in,
    f_ref,
    h_ref,
    row_mem,
    row_lat,
    sums_mem,
    sums_lat,
    send_sem,
    recv_sem,
):
    z = lax.axis_index("lat_0")
    y = lax.axis_index("lat_1")
    x = lax.axis_index("mem_0")
    c = lax.axis_index("mem_1")
    band = z * NYC + y
    mem = x * NC + c

    def lat_peer(k):
        j = k // NYC
        dz = NZ // 2 + ((j + 1) // 2) * (1 - 2 * (j % 2))
        zz = (z + dz) % NZ
        yy = (y + (NYC - 1) - k % NYC) % NYC
        return zz * NYC + yy, {"lat_0": zz, "lat_1": yy}

    def mem_peer(k):
        other = (mem + k) % MEMS
        return other, {"mem_0": other // NC, "mem_1": other % NC}

    barrier = pltpu.get_barrier_semaphore()

    def greet_lat(k, carry):
        pl.semaphore_signal(barrier, inc=1, device_id=lat_peer(k)[1], device_id_type=MESH_ID)
        return carry

    def greet_mem(k, carry):
        pl.semaphore_signal(barrier, inc=1, device_id=mem_peer(k)[1], device_id_type=MESH_ID)
        return carry

    lax.fori_loop(0, BANDS - 1, greet_lat, 0)
    lax.fori_loop(1, MEMS, greet_mem, 0)

    def remote(src, dst, phase, to):
        return pltpu.make_async_remote_copy(
            src_ref=src,
            dst_ref=dst,
            send_sem=send_sem.at[phase],
            recv_sem=recv_sem.at[phase],
            device_id=to,
            device_id_type=MESH_ID,
        )

    def lat_start(src, dst, phase, first=0, last=BANDS - 1):
        def go(k, carry):
            there, to = lat_peer(k)
            remote(src.at[there, pl.ds(0, ROWS)], dst.at[band, pl.ds(0, ROWS)], phase, to).start()
            return carry

        lax.fori_loop(first, last, go, 0)

    def group_start(src, dst, g):
        cols = pl.ds(g * GROUP, GROUP)

        def go(k, carry):
            there, to = lat_peer(k)
            remote(
                src.at[there, pl.ds(0, ROWS), cols], dst.at[band, pl.ds(0, ROWS), cols], UU + g, to
            ).start()
            return carry

        lax.fori_loop(0, BANDS - 1, go, 0)

    def wait_bytes(ref, sem):
        pltpu.make_async_copy(ref, ref, sem).wait()

    def lat_recv(dst, phase):
        wait_bytes(dst.at[pl.ds(0, BANDS - 1), pl.ds(0, ROWS)], recv_sem.at[phase])

    def lat_sent(src, phase):
        wait_bytes(src.at[pl.ds(0, BANDS - 1), pl.ds(0, ROWS)], send_sem.at[phase])

    def clear(buffer):
        shape = (BANDS, PAD - ROWS, buffer.shape[-1])
        buffer[:, ROWS:PAD, :] = jnp.zeros(shape, BF)

    cell = cell_ref[...]
    line = ((cell.astype(F32) + 0.5) * (1.0 / NX)).astype(jnp.int32)
    level = ((line.astype(F32) + 0.5) * (1.0 / ROWS)).astype(jnp.int32)
    col_ref[...] = cell - line * NX - mem * TILE
    line_ref[...] = (line - level * ROWS) * LEV + level

    def scatter(target, with_innovation):
        target[...] = jnp.zeros((LINES, TILE), F32)

        def step(k, carry):
            here = pl.ds(pl.multiple_of(k * CHUNK, CHUNK), CHUNK)
            values = accept_ref[:, here].astype(F32) * prec_ref[:, here]
            if with_innovation:
                values = values * innov_ref[:, here]
            high = values.astype(BF).astype(F32)
            at_line = iota((LINES, CHUNK), 0) == line_ref[:, here]
            at_col = (iota((TILE, CHUNK), 0) == col_ref[:, here]).astype(F32).astype(BF)
            total = target[...]
            for piece in (high, values - high):
                picked = jnp.where(at_line, piece, 0.0).astype(BF)
                total = total + lax.dot_general(
                    picked, at_col, (((1,), (1,)), ((), ())), preferred_element_type=F32
                )
            target[...] = total
            return carry

        lax.fori_loop(0, OBS // CHUNK, step, 0)

    def by_level(values):
        return dot(perm[...], values).astype(BF).reshape(LEV, PAD, values.shape[-1])

    def tile_gather(out, inward, every, phase_lat, phase_mem):
        @pl.when(mem < TILES)
        def _():
            lat_recv(inward, phase_lat)
            inward[band] = out[band]

            def go(k, carry):
                _, to = mem_peer(k)
                remote(
                    inward.at[:, pl.ds(0, ROWS)], every.at[mem, :, pl.ds(0, ROWS)], phase_mem, to
                ).start()
                return carry

            lax.fori_loop(1, MEMS, go, 0)
            every[mem] = inward[...]
            wait_bytes(every.at[pl.ds(0, TILES - 1), :, pl.ds(0, ROWS)], recv_sem.at[phase_mem])

        @pl.when(mem >= TILES)
        def _():
            wait_bytes(every.at[pl.ds(0, TILES), :, pl.ds(0, ROWS)], recv_sem.at[phase_mem])

    def owner_schur(every):
        for t in range(TILES):
            cols = slice(t * TILE, (t + 1) * TILE)
            product = recv_p[:, :, cols].astype(F32) * every[t].astype(F32)
            flat[:, cols] = product.astype(BF).reshape(WIDE, TILE)

    def correlate(target):
        acc[...] = jnp.zeros((WIDE, NX), F32)

        def scale(s, carry):
            rows = dot(lat_tab[s], flat[...]).astype(BF)
            across[:, EDGE : EDGE + NX] = rows
            across[:, :EDGE] = rows[:, NX - EDGE :]
            across[:, EDGE + NX :] = rows[:, :EDGE]
            for first in range(0, NX, BLOCK):
                window = across[:, first : first + BLOCK + 2 * EDGE]
                acc[:, first : first + BLOCK] += sw_ref[s] * dot(window, lon_tab[s])
            return carry

        lax.fori_loop(0, SCALES, scale, 0)
        target[...] = acc[...].astype(BF).reshape(LEV, PAD, NX)

    def mix(tables, source):
        flat[...] = source[...].reshape(WIDE, NX)
        return dot(tables[0], flat[...]) + dot(tables[1], flat[...])

    def build_perm():
        row, col = iota((WIDE, LINES), 0), iota((WIDE, LINES), 1)
        inner = row % PAD
        match = jnp.logical_and(inner < ROWS, inner * LEV + row // PAD == col)
        perm[...] = match.astype(F32).astype(BF)

    def build_tables():
        def lat(s, carry):
            row, col = iota((WIDE, WIDE), 0), iota((WIDE, WIDE), 1)
            valid = jnp.logical_and(row % PAD < ROWS, col % PAD < ROWS)
            gap = (row // PAD - col // PAD) * ROWS + row % PAD - col % PAD
            scaled = gap.astype(F32) / latlen_ref[s]
            lat_tab[s] = jnp.where(valid, jnp.exp(-0.5 * scaled * scaled), 0.0).astype(BF)
            return carry

        lax.fori_loop(0, SCALES, lat, 0)

        def lon(s, carry):
            tall = (BLOCK + 2 * EDGE, BLOCK)
            gap = iota(tall, 0) - EDGE - iota(tall, 1)
            scaled = gap.astype(F32) / lonlen_ref[s]
            lon_tab[s] = jnp.exp(-0.5 * scaled * scaled).astype(BF)
            return carry

        lax.fori_loop(0, SCALES, lon, 0)
        vert = vert_ref[...]
        both = lax.dot_general(
            vert,
            vert,
            (((1,), (1,)), ((), ())),
            precision=lax.Precision.HIGHEST,
            preferred_element_type=F32,
        )
        pick_row = (iota((LINES, LEV), 0) % LEV == iota((LINES, LEV), 1)).astype(F32).astype(BF)
        pick_col = (iota((LEV, WIDE), 1) // PAD == iota((LEV, WIDE), 0)).astype(F32).astype(BF)
        same = iota((LINES, WIDE), 0) // LEV == iota((LINES, WIDE), 1) % PAD
        for matrix, target in ((vert.T, grad_mix), (both, image_mix)):
            high = matrix.astype(BF)
            low = (matrix - high.astype(F32)).astype(BF)
            for index, piece in enumerate((high, low)):
                rows = dot(pick_row, piece).astype(BF)
                target[index] = jnp.where(same, -dot(rows, pick_col), 0.0).astype(BF)

    def pert():
        return pert_ref[...].astype(F32).reshape(LINES, NX)

    for buffer in (recv_p, recv_t, recv_u, recv_r):
        clear(buffer)
    for buffer in (tile_in, tile_in_two):
        clear(buffer)
    for every in (tiles, tiles_two):
        for t in range(TILES):
            clear(every.at[t])
    build_perm()
    scatter(spread, True)
    tile_out[...] = by_level(spread[...].astype(BF))
    pl.semaphore_wait(barrier, BANDS - 1 + MEMS - 1)

    @pl.when(mem < TILES)
    def _():
        lat_start(tile_out, tile_in, S1)

    send_p[...] = by_level(pert_ref[...].reshape(LINES, NX))
    lat_start(send_p, recv_p, PP)
    build_tables()
    tile_gather(tile_out, tile_in, tiles, S1, A1)
    scatter(weight, False)
    recv_p[band] = send_p[band]
    lat_recv(recv_p, PP)
    owner_schur(tiles)
    correlate(send_t)
    lat_start(send_t, recv_t, TT, 0, EARLY)
    flat[...] = send_t[...].reshape(WIDE, NX)
    correlate(send_u)
    for g in range(GROUPS):
        group_start(send_u, recv_u, g)
    recv_u[band] = send_u[band]
    recv_t[band] = send_t[band]

    def image_step():
        part_in[mem] = part[mem]
        wait_bytes(part_in.at[pl.ds(0, MEMS - 1)], recv_sem.at[RS])
        image = jnp.sum(part_in[...].astype(F32), axis=0)
        weighted = weight[...] * image
        spread[...] = weighted * image
        tile_out_two[...] = by_level(weighted.astype(BF))
        lat_start(tile_out_two, tile_in_two, S2)

    for g in range(GROUPS):
        cols = slice(g * GROUP, (g + 1) * GROUP)
        wait_bytes(recv_u.at[pl.ds(0, BANDS - 1), pl.ds(0, ROWS), cols], recv_sem.at[UU + g])
        got = recv_u[:, :, cols].reshape(WIDE, GROUP)
        mixed = dot(image_mix[0], got) + dot(image_mix[1], got)
        partial = (pert_ref[:, :, cols].astype(F32).reshape(LINES, GROUP) * mixed).astype(BF)
        for half in range(NC):
            t = g * NC + half
            part[t] = partial[:, half * TILE : (half + 1) * TILE]

            @pl.when(mem != t)
            def _():
                to = {"mem_0": g, "mem_1": half}
                remote(part.at[t], part_in.at[mem], RS, to).start()

        if g > 0:
            pl.when(x == g - 1)(image_step)

    @pl.when(x == GROUPS - 1)
    def _():
        lat_start(send_t, recv_t, TT, EARLY, NEAR)
        image_step()
        lat_start(send_t, recv_t, TT, NEAR, BANDS - 1)

    @pl.when(x != GROUPS - 1)
    def _():
        lat_start(send_t, recv_t, TT, EARLY, BANDS - 1)

    @pl.when(mem >= TILES)
    def _():
        spread[...] = jnp.zeros((LINES, TILE), F32)

    obs_square = jnp.sum(spread[...])
    tile_gather(tile_out_two, tile_in_two, tiles_two, S2, A2)
    owner_schur(tiles_two)
    correlate(send_r)
    lat_start(send_r, recv_r, RR)
    recv_r[band] = send_r[band]
    lat_recv(recv_t, TT)
    f_ref[...] = mix(grad_mix, recv_t)
    grad_square = jnp.sum(f_ref[...] * f_ref[...])
    lat_recv(recv_r, RR)
    h_ref[...] = -mix(grad_mix, recv_r)
    cross = jnp.sum(f_ref[...] * h_ref[...])
    hess_square = jnp.sum(h_ref[...] * h_ref[...])

    lane = iota((1, 128), 1)
    row = jnp.zeros((1, 128), F32)
    for index, value in enumerate((grad_square, cross, hess_square, obs_square)):
        row = jnp.where(lane == index, value, row)
    row_mem[...] = row

    def tell_mem(k, carry):
        _, to = mem_peer(k)
        remote(row_mem, sums_mem.at[mem], SM, to).start()
        return carry

    lax.fori_loop(1, MEMS, tell_mem, 0)
    sums_mem[mem] = row
    wait_bytes(sums_mem.at[pl.ds(0, MEMS - 1)], recv_sem.at[SM])
    row = jnp.sum(sums_mem[...], axis=0)
    row_lat[...] = row

    def tell_lat(k, carry):
        _, to = lat_peer(k)
        remote(row_lat, sums_lat.at[band], SL, to).start()
        return carry

    lax.fori_loop(0, BANDS - 1, tell_lat, 0)
    sums_lat[band] = row
    wait_bytes(sums_lat.at[pl.ds(0, BANDS - 1)], recv_sem.at[SL])
    total = jnp.sum(sums_lat[...], axis=0)
    grad_square, cross, hess_square, obs_square = (
        jnp.sum(jnp.where(lane == index, total, 0.0)) for index in range(4)
    )
    first_step = grad_square / (grad_square + obs_square)
    second_step = (grad_square + cross) / (grad_square + 2.0 * cross + hess_square)
    gradient = f_ref[...] - first_step * (f_ref[...] + h_ref[...])
    gradient_ref[...] = gradient
    control_ref[...] = -first_step * f_ref[...] - second_step * gradient

    for buffer, phase in ((send_p, PP), (send_t, TT), (send_r, RR)):
        lat_sent(buffer, phase)
    for g in range(GROUPS):
        cols = slice(g * GROUP, (g + 1) * GROUP)
        wait_bytes(send_u.at[pl.ds(0, BANDS - 1), pl.ds(0, ROWS), cols], send_sem.at[UU + g])

    @pl.when(mem < TILES)
    def _():
        lat_sent(tile_out, S1)
        lat_sent(tile_out_two, S2)
        for every, phase in ((tiles, A1), (tiles_two, A2)):
            wait_bytes(every.at[pl.ds(0, MEMS - 1), :, pl.ds(0, ROWS)], send_sem.at[phase])
        wait_bytes(part_in.at[pl.ds(0, TILES - 1)], send_sem.at[RS])

    @pl.when(mem >= TILES)
    def _():
        wait_bytes(part_in.at[pl.ds(0, TILES)], send_sem.at[RS])

    wait_bytes(sums_mem.at[pl.ds(0, MEMS - 1)], send_sem.at[SM])
    wait_bytes(sums_lat.at[pl.ds(0, BANDS - 1)], send_sem.at[SL])


def local(
    ens_perts,
    vert_loc,
    lat_lengths,
    lon_lengths,
    scale_weights,
    obs_cell,
    obs_accept,
    innovation,
    obs_precision,
):
    vmem = pl.BlockSpec(memory_space=pltpu.VMEM)
    smem = pl.BlockSpec(memory_space=pltpu.SMEM)
    slab = pltpu.VMEM((BANDS, PAD, NX), BF)
    lines = pltpu.VMEM((LINES, NX), F32)
    chunk = pltpu.VMEM((LINES, TILE), F32)
    level_tile = pltpu.VMEM((BANDS, PAD, TILE), BF)
    all_tiles = pltpu.VMEM((MEMS, BANDS, PAD, TILE), BF)
    new_control, gradient = pl.pallas_call(
        kernel,
        out_shape=(
            jax.ShapeDtypeStruct((LINES, NX), F32),
            jax.ShapeDtypeStruct((LINES, NX), F32),
        ),
        in_specs=[vmem, vmem, smem, smem, smem, vmem, vmem, vmem, vmem],
        out_specs=(vmem, vmem),
        scratch_shapes=[
            pltpu.VMEM((WIDE, LINES), BF),
            pltpu.VMEM((SCALES, WIDE, WIDE), BF),
            pltpu.VMEM((SCALES, BLOCK + 2 * EDGE, BLOCK), BF),
            pltpu.VMEM((2, LINES, WIDE), BF),
            pltpu.VMEM((2, LINES, WIDE), BF),
            pltpu.VMEM((1, OBS), jnp.int32),
            pltpu.VMEM((1, OBS), jnp.int32),
            chunk,
            chunk,
            pltpu.VMEM((WIDE, NX), F32),
            pltpu.VMEM((WIDE, NX + 2 * EDGE), BF),
            pltpu.VMEM((WIDE, NX), BF),
            slab,
            slab,
            slab,
            slab,
            slab,
            slab,
            slab,
            slab,
            level_tile,
            level_tile,
            all_tiles,
            level_tile,
            level_tile,
            all_tiles,
            pltpu.VMEM((TILES, LINES, TILE), BF),
            pltpu.VMEM((MEMS, LINES, TILE), BF),
            lines,
            lines,
            pltpu.VMEM((1, 128), F32),
            pltpu.VMEM((1, 128), F32),
            pltpu.VMEM((MEMS, 1, 128), F32),
            pltpu.VMEM((BANDS, 1, 128), F32),
            pltpu.SemaphoreType.DMA((10 + GROUPS,)),
            pltpu.SemaphoreType.DMA((10 + GROUPS,)),
        ],
        compiler_params=pltpu.CompilerParams(
            collective_id=0, has_side_effects=True, vmem_limit_bytes=62 * 1024 * 1024
        ),
    )(
        ens_perts[0].transpose(1, 0, 2),
        vert_loc,
        lat_lengths,
        lon_lengths,
        scale_weights,
        obs_cell.reshape(1, OBS),
        obs_accept.reshape(1, OBS),
        innovation.reshape(1, OBS),
        obs_precision.reshape(1, OBS),
    )

    def placed(field):
        return field.reshape(ROWS, LEV, NX).transpose(1, 0, 2)[None]

    return (placed(new_control), placed(gradient))


def solution(mesh):
    split = Mesh(mesh.devices.reshape(NZ, NYC, NXC, NC), ("lat_0", "lat_1", "mem_0", "mem_1"))
    placed = (P(MEM, None, LAT, None), P(), P(), P(), P(), P(LAT), P(LAT), P(LAT), P(LAT))
    return jax.shard_map(
        local,
        mesh=split,
        in_specs=placed,
        out_specs=(P(MEM, None, LAT, None), P(MEM, None, LAT, None)),
        check_vma=False,
    )
```

```python
import jax
import jax.numpy as jnp
from jax import lax
from jax.experimental import pallas as pl
from jax.experimental.pallas import tpu as pltpu
from jax.sharding import Mesh
from jax.sharding import PartitionSpec as P

LAT = ("lat_0", "lat_1")
MEM = ("mem_0", "mem_1")
MESH_ID = pl.DeviceIdType.MESH
NZ, NYC, NXC, NC = 16, 4, 4, 2
BANDS = NZ * NYC
MEMS = NXC * NC
LEV = 64
ROWS = 6
PAD = 8
NX = 768
LINES = ROWS * LEV
WIDE = LEV * PAD
SCALES = 3
OBS = 8192
BLOCK = 256
EDGE = 128
TILE = 128
TILES = NX // TILE
GROUP = 256
GROUPS = NX // GROUP
EARLY = 4
NEAR = 8
TAIL = 40
CHUNK = 512
BF = jnp.bfloat16
F32 = jnp.float32

PP, S1, A1, B1, TT, RS, S2, A2, B2, RR, SM, SL, UU = range(13)


def iota(shape, dim):
    return lax.broadcasted_iota(jnp.int32, shape, dim)


def dot(a, b):
    return jnp.dot(a, b, preferred_element_type=F32)


def kernel(
    pert_ref,
    vert_ref,
    latlen_ref,
    lonlen_ref,
    sw_ref,
    cell_ref,
    accept_ref,
    innov_ref,
    prec_ref,
    control_ref,
    gradient_ref,
    perm,
    lat_tab,
    lon_tab,
    grad_mix,
    image_mix,
    line_ref,
    col_ref,
    spread,
    weight,
    acc,
    across,
    flat,
    send_p,
    send_t,
    send_u,
    send_r,
    recv_p,
    recv_t,
    recv_u,
    recv_r,
    tile_out,
    tile_in,
    tiles,
    tile_out_two,
    tile_in_two,
    tiles_two,
    part,
    part_in,
    f_ref,
    h_ref,
    stats,
    row_mem,
    row_lat,
    sums_mem,
    sums_lat,
    send_sem,
    recv_sem,
):
    z = lax.axis_index("lat_0")
    y = lax.axis_index("lat_1")
    x = lax.axis_index("mem_0")
    c = lax.axis_index("mem_1")
    band = z * NYC + y
    mem = x * NC + c

    def lat_peer(k):
        j = k // NYC
        dz = NZ // 2 + ((j + 1) // 2) * (1 - 2 * (j % 2))
        zz = (z + dz) % NZ
        yy = (y + (NYC - 1) - k % NYC) % NYC
        return zz * NYC + yy, {"lat_0": zz, "lat_1": yy}

    def mem_peer(k):
        other = (mem + k) % MEMS
        return other, {"mem_0": other // NC, "mem_1": other % NC}

    barrier = pltpu.get_barrier_semaphore()

    def greet_lat(k, carry):
        pl.semaphore_signal(barrier, inc=1, device_id=lat_peer(k)[1], device_id_type=MESH_ID)
        return carry

    def greet_mem(k, carry):
        pl.semaphore_signal(barrier, inc=1, device_id=mem_peer(k)[1], device_id_type=MESH_ID)
        return carry

    lax.fori_loop(0, BANDS - 1, greet_lat, 0)
    lax.fori_loop(1, MEMS, greet_mem, 0)

    def remote(src, dst, phase, to):
        return pltpu.make_async_remote_copy(
            src_ref=src,
            dst_ref=dst,
            send_sem=send_sem.at[phase],
            recv_sem=recv_sem.at[phase],
            device_id=to,
            device_id_type=MESH_ID,
        )

    def lat_start(src, dst, phase, first=0, last=BANDS - 1):
        def go(k, carry):
            there, to = lat_peer(k)
            remote(src.at[there, pl.ds(0, ROWS)], dst.at[band, pl.ds(0, ROWS)], phase, to).start()
            return carry

        lax.fori_loop(first, last, go, 0)

    def group_start(src, dst, g):
        cols = pl.ds(g * GROUP, GROUP)

        def go(k, carry):
            there, to = lat_peer(k)
            remote(
                src.at[there, pl.ds(0, ROWS), cols], dst.at[band, pl.ds(0, ROWS), cols], UU + g, to
            ).start()
            return carry

        lax.fori_loop(0, BANDS - 1, go, 0)

    def wait_bytes(ref, sem):
        pltpu.make_async_copy(ref, ref, sem).wait()

    def lat_recv(dst, phase):
        wait_bytes(dst.at[pl.ds(0, BANDS - 1), pl.ds(0, ROWS)], recv_sem.at[phase])

    def lat_sent(src, phase):
        wait_bytes(src.at[pl.ds(0, BANDS - 1), pl.ds(0, ROWS)], send_sem.at[phase])

    def clear(buffer):
        shape = (BANDS, PAD - ROWS, buffer.shape[-1])
        buffer[:, ROWS:PAD, :] = jnp.zeros(shape, BF)

    cell = cell_ref[...]
    line = ((cell.astype(F32) + 0.5) * (1.0 / NX)).astype(jnp.int32)
    level = ((line.astype(F32) + 0.5) * (1.0 / ROWS)).astype(jnp.int32)
    col_ref[...] = cell - line * NX - mem * TILE
    line_ref[...] = (line - level * ROWS) * LEV + level

    def scatter(target, with_innovation):
        target[...] = jnp.zeros((LINES, TILE), F32)

        def step(k, carry):
            here = pl.ds(pl.multiple_of(k * CHUNK, CHUNK), CHUNK)
            values = accept_ref[:, here].astype(F32) * prec_ref[:, here]
            if with_innovation:
                values = values * innov_ref[:, here]
            high = values.astype(BF).astype(F32)
            at_line = iota((LINES, CHUNK), 0) == line_ref[:, here]
            at_col = (iota((TILE, CHUNK), 0) == col_ref[:, here]).astype(F32).astype(BF)
            total = target[...]
            for piece in (high, values - high):
                picked = jnp.where(at_line, piece, 0.0).astype(BF)
                total = total + lax.dot_general(
                    picked, at_col, (((1,), (1,)), ((), ())), preferred_element_type=F32
                )
            target[...] = total
            return carry

        lax.fori_loop(0, OBS // CHUNK, step, 0)

    def by_level(values):
        return dot(perm[...], values).astype(BF).reshape(LEV, PAD, values.shape[-1])

    def tile_gather(out, inward, every, phase_lat, phase_chip, phase_pair):
        partner = {"mem_1": 1 - c}

        def of(tile):
            return every.at[tile, :, pl.ds(0, ROWS)]

        def chips(count):
            return every.at[pl.ds(0, count), :, pl.ds(0, ROWS)]

        @pl.when(mem < TILES)
        def _():
            lat_recv(inward, phase_lat)
            inward[band] = out[band]
            mine = inward.at[:, pl.ds(0, ROWS)]
            for k in range(1, NXC):
                remote(mine, of(mem), phase_chip, {"mem_0": (x + k) % NXC}).start()
            remote(mine, of(mem), phase_pair, partner).start()
            every[mem] = inward[...]
            wait_bytes(chips(GROUPS - 1), recv_sem.at[phase_chip])

        @pl.when(mem >= TILES)
        def _():
            wait_bytes(chips(GROUPS), recv_sem.at[phase_chip])

        for g in range(GROUPS):

            @pl.when(x != g)
            def _():
                there = g * NC + c
                remote(of(there), of(there), phase_pair, partner).start()

        wait_bytes(chips(GROUPS), recv_sem.at[phase_pair])

    def owner_schur(every):
        for t in range(TILES):
            cols = slice(t * TILE, (t + 1) * TILE)
            product = recv_p[:, :, cols].astype(F32) * every[t].astype(F32)
            flat[:, cols] = product.astype(BF).reshape(WIDE, TILE)

    def correlate(target):
        acc[...] = jnp.zeros((WIDE, NX), F32)

        def scale(s, carry):
            rows = dot(lat_tab[s], flat[...]).astype(BF)
            across[:, EDGE : EDGE + NX] = rows
            across[:, :EDGE] = rows[:, NX - EDGE :]
            across[:, EDGE + NX :] = rows[:, :EDGE]
            for first in range(0, NX, BLOCK):
                window = across[:, first : first + BLOCK + 2 * EDGE]
                acc[:, first : first + BLOCK] += sw_ref[s] * dot(window, lon_tab[s])
            return carry

        lax.fori_loop(0, SCALES, scale, 0)
        target[...] = acc[...].astype(BF).reshape(LEV, PAD, NX)

    def mix(tables, source):
        flat[...] = source[...].reshape(WIDE, NX)
        return dot(tables[0], flat[...]) + dot(tables[1], flat[...])

    def build_perm():
        row, col = iota((WIDE, LINES), 0), iota((WIDE, LINES), 1)
        inner = row % PAD
        match = jnp.logical_and(inner < ROWS, inner * LEV + row // PAD == col)
        perm[...] = match.astype(F32).astype(BF)

    def build_tables():
        def lat(s, carry):
            row, col = iota((WIDE, WIDE), 0), iota((WIDE, WIDE), 1)
            valid = jnp.logical_and(row % PAD < ROWS, col % PAD < ROWS)
            gap = (row // PAD - col // PAD) * ROWS + row % PAD - col % PAD
            scaled = gap.astype(F32) / latlen_ref[s]
            lat_tab[s] = jnp.where(valid, jnp.exp(-0.5 * scaled * scaled), 0.0).astype(BF)
            return carry

        lax.fori_loop(0, SCALES, lat, 0)

        def lon(s, carry):
            tall = (BLOCK + 2 * EDGE, BLOCK)
            gap = iota(tall, 0) - EDGE - iota(tall, 1)
            scaled = gap.astype(F32) / lonlen_ref[s]
            lon_tab[s] = jnp.exp(-0.5 * scaled * scaled).astype(BF)
            return carry

        lax.fori_loop(0, SCALES, lon, 0)
        vert = vert_ref[...]
        both = lax.dot_general(
            vert,
            vert,
            (((1,), (1,)), ((), ())),
            precision=lax.Precision.HIGHEST,
            preferred_element_type=F32,
        )
        pick_row = (iota((LINES, LEV), 0) % LEV == iota((LINES, LEV), 1)).astype(F32).astype(BF)
        pick_col = (iota((LEV, WIDE), 1) // PAD == iota((LEV, WIDE), 0)).astype(F32).astype(BF)
        same = iota((LINES, WIDE), 0) // LEV == iota((LINES, WIDE), 1) % PAD
        for matrix, target in ((vert.T, grad_mix), (both, image_mix)):
            high = matrix.astype(BF)
            low = (matrix - high.astype(F32)).astype(BF)
            for index, piece in enumerate((high, low)):
                rows = dot(pick_row, piece).astype(BF)
                target[index] = jnp.where(same, -dot(rows, pick_col), 0.0).astype(BF)

    def pert():
        return pert_ref[...].astype(F32).reshape(LINES, NX)

    for buffer in (recv_p, recv_t, recv_u, recv_r):
        clear(buffer)
    for buffer in (tile_in, tile_in_two):
        clear(buffer)
    for every in (tiles, tiles_two):
        for t in range(TILES):
            clear(every.at[t])
    lane = iota((1, 128), 1)
    stats[...] = jnp.zeros((1, 128), F32)
    build_perm()
    scatter(spread, True)
    tile_out[...] = by_level(spread[...].astype(BF))
    pl.semaphore_wait(barrier, BANDS - 1 + MEMS - 1)

    @pl.when(mem < TILES)
    def _():
        lat_start(tile_out, tile_in, S1)

    send_p[...] = by_level(pert_ref[...].reshape(LINES, NX))
    lat_start(send_p, recv_p, PP)
    build_tables()
    tile_gather(tile_out, tile_in, tiles, S1, A1, B1)
    scatter(weight, False)
    recv_p[band] = send_p[band]
    lat_recv(recv_p, PP)
    owner_schur(tiles)
    correlate(send_t)
    lat_start(send_t, recv_t, TT, 0, EARLY)
    flat[...] = send_t[...].reshape(WIDE, NX)
    correlate(send_u)
    for g in range(GROUPS):
        group_start(send_u, recv_u, g)
    recv_u[band] = send_u[band]
    recv_t[band] = send_t[band]

    def image_step():
        part_in[mem] = part[mem]
        wait_bytes(part_in.at[pl.ds(0, MEMS - 1)], recv_sem.at[RS])
        image = jnp.sum(part_in[...].astype(F32), axis=0)
        weighted = weight[...] * image
        square = jnp.sum(weighted * image)
        first = -jnp.sum(spread[...] * image)
        stats[...] = jnp.where(lane == 0, first, jnp.where(lane == 1, square, 0.0))
        tile_out_two[...] = by_level(weighted.astype(BF))
        lat_start(tile_out_two, tile_in_two, S2)

    for g in range(GROUPS):
        cols = slice(g * GROUP, (g + 1) * GROUP)
        wait_bytes(recv_u.at[pl.ds(0, BANDS - 1), pl.ds(0, ROWS), cols], recv_sem.at[UU + g])
        got = recv_u[:, :, cols].reshape(WIDE, GROUP)
        mixed = dot(image_mix[0], got) + dot(image_mix[1], got)
        partial = (pert_ref[:, :, cols].astype(F32).reshape(LINES, GROUP) * mixed).astype(BF)
        for half in range(NC):
            t = g * NC + half
            part[t] = partial[:, half * TILE : (half + 1) * TILE]

            @pl.when(mem != t)
            def _():
                to = {"mem_0": g, "mem_1": half}
                remote(part.at[t], part_in.at[mem], RS, to).start()

        if g > 0:
            pl.when(x == g - 1)(image_step)

    @pl.when(x == GROUPS - 1)
    def _():
        lat_start(send_t, recv_t, TT, EARLY, NEAR)
        image_step()
        lat_start(send_t, recv_t, TT, NEAR, TAIL)

    @pl.when(x != GROUPS - 1)
    def _():
        lat_start(send_t, recv_t, TT, EARLY, TAIL)

    tile_gather(tile_out_two, tile_in_two, tiles_two, S2, A2, B2)
    owner_schur(tiles_two)
    correlate(send_r)
    lat_start(send_r, recv_r, RR)
    lat_start(send_t, recv_t, TT, TAIL, BANDS - 1)
    recv_r[band] = send_r[band]
    lat_recv(recv_r, RR)
    h_ref[...] = -mix(grad_mix, recv_r)
    row = jnp.where(lane == 2, jnp.sum(h_ref[...] * h_ref[...]), stats[...])
    row_mem[...] = row

    def tell_mem(k, carry):
        _, to = mem_peer(k)
        remote(row_mem, sums_mem.at[mem], SM, to).start()
        return carry

    lax.fori_loop(1, MEMS, tell_mem, 0)
    sums_mem[mem] = row
    wait_bytes(sums_mem.at[pl.ds(0, MEMS - 1)], recv_sem.at[SM])
    row = jnp.sum(sums_mem[...], axis=0)
    row_lat[...] = row

    def tell_lat(k, carry):
        _, to = lat_peer(k)
        remote(row_lat, sums_lat.at[band], SL, to).start()
        return carry

    lax.fori_loop(0, BANDS - 1, tell_lat, 0)
    sums_lat[band] = row
    lat_recv(recv_t, TT)
    f_ref[...] = mix(grad_mix, recv_t)
    wait_bytes(sums_lat.at[pl.ds(0, BANDS - 1)], recv_sem.at[SL])
    total = jnp.sum(sums_lat[...], axis=0)
    grad_square, obs_square, hess_square = (
        jnp.sum(jnp.where(lane == index, total, 0.0)) for index in range(3)
    )
    first_step = grad_square / (grad_square + obs_square)
    second_step = (grad_square + obs_square) / (grad_square + 2.0 * obs_square + hess_square)
    gradient = f_ref[...] - first_step * (f_ref[...] + h_ref[...])
    gradient_ref[...] = gradient
    control_ref[...] = -first_step * f_ref[...] - second_step * gradient

    for buffer, phase in ((send_p, PP), (send_t, TT), (send_r, RR)):
        lat_sent(buffer, phase)
    for g in range(GROUPS):
        cols = slice(g * GROUP, (g + 1) * GROUP)
        wait_bytes(send_u.at[pl.ds(0, BANDS - 1), pl.ds(0, ROWS), cols], send_sem.at[UU + g])

    @pl.when(mem < TILES)
    def _():
        lat_sent(tile_out, S1)
        lat_sent(tile_out_two, S2)
        for every, phase in ((tiles, A1), (tiles_two, A2)):
            wait_bytes(every.at[pl.ds(0, NXC - 1), :, pl.ds(0, ROWS)], send_sem.at[phase])
        wait_bytes(part_in.at[pl.ds(0, TILES - 1)], send_sem.at[RS])

    for every, phase in ((tiles, B1), (tiles_two, B2)):
        wait_bytes(every.at[pl.ds(0, GROUPS), :, pl.ds(0, ROWS)], send_sem.at[phase])

    @pl.when(mem >= TILES)
    def _():
        wait_bytes(part_in.at[pl.ds(0, TILES)], send_sem.at[RS])

    wait_bytes(sums_mem.at[pl.ds(0, MEMS - 1)], send_sem.at[SM])
    wait_bytes(sums_lat.at[pl.ds(0, BANDS - 1)], send_sem.at[SL])


def local(
    ens_perts,
    vert_loc,
    lat_lengths,
    lon_lengths,
    scale_weights,
    obs_cell,
    obs_accept,
    innovation,
    obs_precision,
):
    vmem = pl.BlockSpec(memory_space=pltpu.VMEM)
    smem = pl.BlockSpec(memory_space=pltpu.SMEM)
    slab = pltpu.VMEM((BANDS, PAD, NX), BF)
    lines = pltpu.VMEM((LINES, NX), F32)
    chunk = pltpu.VMEM((LINES, TILE), F32)
    level_tile = pltpu.VMEM((BANDS, PAD, TILE), BF)
    all_tiles = pltpu.VMEM((MEMS, BANDS, PAD, TILE), BF)
    new_control, gradient = pl.pallas_call(
        kernel,
        out_shape=(
            jax.ShapeDtypeStruct((LINES, NX), F32),
            jax.ShapeDtypeStruct((LINES, NX), F32),
        ),
        in_specs=[vmem, vmem, smem, smem, smem, vmem, vmem, vmem, vmem],
        out_specs=(vmem, vmem),
        scratch_shapes=[
            pltpu.VMEM((WIDE, LINES), BF),
            pltpu.VMEM((SCALES, WIDE, WIDE), BF),
            pltpu.VMEM((SCALES, BLOCK + 2 * EDGE, BLOCK), BF),
            pltpu.VMEM((2, LINES, WIDE), BF),
            pltpu.VMEM((2, LINES, WIDE), BF),
            pltpu.VMEM((1, OBS), jnp.int32),
            pltpu.VMEM((1, OBS), jnp.int32),
            chunk,
            chunk,
            pltpu.VMEM((WIDE, NX), F32),
            pltpu.VMEM((WIDE, NX + 2 * EDGE), BF),
            pltpu.VMEM((WIDE, NX), BF),
            slab,
            slab,
            slab,
            slab,
            slab,
            slab,
            slab,
            slab,
            level_tile,
            level_tile,
            all_tiles,
            level_tile,
            level_tile,
            all_tiles,
            pltpu.VMEM((TILES, LINES, TILE), BF),
            pltpu.VMEM((MEMS, LINES, TILE), BF),
            lines,
            lines,
            pltpu.VMEM((1, 128), F32),
            pltpu.VMEM((1, 128), F32),
            pltpu.VMEM((1, 128), F32),
            pltpu.VMEM((MEMS, 1, 128), F32),
            pltpu.VMEM((BANDS, 1, 128), F32),
            pltpu.SemaphoreType.DMA((12 + GROUPS,)),
            pltpu.SemaphoreType.DMA((12 + GROUPS,)),
        ],
        compiler_params=pltpu.CompilerParams(
            collective_id=0, has_side_effects=True, vmem_limit_bytes=62 * 1024 * 1024
        ),
    )(
        ens_perts[0].transpose(1, 0, 2),
        vert_loc,
        lat_lengths,
        lon_lengths,
        scale_weights,
        obs_cell.reshape(1, OBS),
        obs_accept.reshape(1, OBS),
        innovation.reshape(1, OBS),
        obs_precision.reshape(1, OBS),
    )

    def placed(field):
        return field.reshape(ROWS, LEV, NX).transpose(1, 0, 2)[None]

    return (placed(new_control), placed(gradient))


def solution(mesh):
    split = Mesh(mesh.devices.reshape(NZ, NYC, NXC, NC), ("lat_0", "lat_1", "mem_0", "mem_1"))
    placed = (P(MEM, None, LAT, None), P(), P(), P(), P(), P(LAT), P(LAT), P(LAT), P(LAT))
    return jax.shard_map(
        local,
        mesh=split,
        in_specs=placed,
        out_specs=(P(MEM, None, LAT, None), P(MEM, None, LAT, None)),
        check_vma=False,
    )
```

```python
import jax
import jax.numpy as jnp
from jax import lax
from jax.experimental import pallas as pl
from jax.experimental.pallas import tpu as pltpu
from jax.sharding import Mesh
from jax.sharding import PartitionSpec as P

LAT = ("lat_0", "lat_1")
MEM = ("mem_0", "mem_1")
MESH_ID = pl.DeviceIdType.MESH
NZ, NYC, NXC, NC = 16, 4, 4, 2
BANDS = NZ * NYC
MEMS = NXC * NC
LEV = 64
ROWS = 6
PAD = 8
NX = 768
LINES = ROWS * LEV
WIDE = LEV * PAD
SCALES = 3
OBS = 8192
EDGE = 128
TILE = 128
TILES = NX // TILE
GROUP = 256
GROUPS = NX // GROUP
EARLY = 4
NEAR = 8
TAIL = 40
CHUNK = 512
BF = jnp.bfloat16
F32 = jnp.float32

PP, S1, A1, B1, TT, RS, S2, A2, B2, SM, SL, UU = range(12)
RR = UU + 3


def iota(shape, dim):
    return lax.broadcasted_iota(jnp.int32, shape, dim)


def dot(a, b):
    return jnp.dot(a, b, preferred_element_type=F32)


def kernel(
    pert_ref,
    vert_ref,
    latlen_ref,
    lonlen_ref,
    sw_ref,
    cell_ref,
    accept_ref,
    innov_ref,
    prec_ref,
    f_out,
    h_out,
    first_ref,
    second_ref,
    perm,
    lat_tab,
    lon_tab,
    grad_mix,
    image_mix,
    line_ref,
    col_ref,
    spread,
    weight,
    across,
    flat,
    send_p,
    send_t,
    send_u,
    send_r,
    recv_p,
    recv_t,
    recv_u,
    recv_r,
    tile_out,
    tile_in,
    tiles,
    tile_out_two,
    tile_in_two,
    tiles_two,
    part,
    part_in,
    f_ref,
    h_ref,
    stats,
    row_mem,
    row_lat,
    sums_mem,
    sums_lat,
    send_sem,
    recv_sem,
    out_sem,
):
    z = lax.axis_index("lat_0")
    y = lax.axis_index("lat_1")
    x = lax.axis_index("mem_0")
    c = lax.axis_index("mem_1")
    band = z * NYC + y
    mem = x * NC + c

    def lat_peer(k):
        j = k // NYC
        dz = NZ // 2 + ((j + 1) // 2) * (1 - 2 * (j % 2))
        zz = (z + dz) % NZ
        yy = (y + (NYC - 1) - k % NYC) % NYC
        return zz * NYC + yy, {"lat_0": zz, "lat_1": yy}

    def mem_peer(k):
        other = (mem + k) % MEMS
        return other, {"mem_0": other // NC, "mem_1": other % NC}

    barrier = pltpu.get_barrier_semaphore()

    def greet_lat(k, carry):
        pl.semaphore_signal(barrier, inc=1, device_id=lat_peer(k)[1], device_id_type=MESH_ID)
        return carry

    def greet_mem(k, carry):
        pl.semaphore_signal(barrier, inc=1, device_id=mem_peer(k)[1], device_id_type=MESH_ID)
        return carry

    lax.fori_loop(0, BANDS - 1, greet_lat, 0)
    lax.fori_loop(1, MEMS, greet_mem, 0)

    def remote(src, dst, phase, to):
        return pltpu.make_async_remote_copy(
            src_ref=src,
            dst_ref=dst,
            send_sem=send_sem.at[phase],
            recv_sem=recv_sem.at[phase],
            device_id=to,
            device_id_type=MESH_ID,
        )

    def lat_start(src, dst, phase, first=0, last=BANDS - 1):
        def go(k, carry):
            there, to = lat_peer(k)
            remote(src.at[there, pl.ds(0, ROWS)], dst.at[band, pl.ds(0, ROWS)], phase, to).start()
            return carry

        lax.fori_loop(first, last, go, 0)

    def group_start(src, dst, phase):
        def start(g):
            cols = pl.ds(g * GROUP, GROUP)

            def go(k, carry):
                there, to = lat_peer(k)
                here = src.at[there, pl.ds(0, ROWS), cols]
                remote(here, dst.at[band, pl.ds(0, ROWS), cols], phase + g, to).start()
                return carry

            lax.fori_loop(0, BANDS - 1, go, 0)

        return start

    def group_bytes(ref, g, sem):
        cols = pl.ds(g * GROUP, GROUP)
        wait_bytes(ref.at[pl.ds(0, BANDS - 1), pl.ds(0, ROWS), cols], sem)

    def wait_bytes(ref, sem):
        pltpu.make_async_copy(ref, ref, sem).wait()

    def lat_recv(dst, phase):
        wait_bytes(dst.at[pl.ds(0, BANDS - 1), pl.ds(0, ROWS)], recv_sem.at[phase])

    def lat_sent(src, phase):
        wait_bytes(src.at[pl.ds(0, BANDS - 1), pl.ds(0, ROWS)], send_sem.at[phase])

    def clear(buffer):
        shape = (BANDS, PAD - ROWS, buffer.shape[-1])
        buffer[:, ROWS:PAD, :] = jnp.zeros(shape, BF)

    cell = cell_ref[...]
    line = ((cell.astype(F32) + 0.5) * (1.0 / NX)).astype(jnp.int32)
    level = ((line.astype(F32) + 0.5) * (1.0 / ROWS)).astype(jnp.int32)
    col_ref[...] = cell - line * NX - mem * TILE
    line_ref[...] = (line - level * ROWS) * LEV + level

    def scatter(target, with_innovation):
        target[...] = jnp.zeros((LINES, TILE), F32)

        def step(k, carry):
            here = pl.ds(pl.multiple_of(k * CHUNK, CHUNK), CHUNK)
            values = accept_ref[:, here].astype(F32) * prec_ref[:, here]
            if with_innovation:
                values = values * innov_ref[:, here]
            high = values.astype(BF).astype(F32)
            at_line = iota((LINES, CHUNK), 0) == line_ref[:, here]
            at_col = (iota((TILE, CHUNK), 0) == col_ref[:, here]).astype(F32).astype(BF)
            total = target[...]
            for piece in (high,) if with_innovation else (high, values - high):
                picked = jnp.where(at_line, piece, 0.0).astype(BF)
                total = total + lax.dot_general(
                    picked, at_col, (((1,), (1,)), ((), ())), preferred_element_type=F32
                )
            target[...] = total
            return carry

        lax.fori_loop(0, OBS // CHUNK, step, 0)

    def by_level(values):
        return dot(perm[...], values).astype(BF).reshape(LEV, PAD, values.shape[-1])

    def tile_gather(out, inward, every, phase_lat, phase_chip, phase_pair):
        partner = {"mem_1": 1 - c}

        def of(tile):
            return every.at[tile, :, pl.ds(0, ROWS)]

        def chips(count):
            return every.at[pl.ds(0, count), :, pl.ds(0, ROWS)]

        @pl.when(mem < TILES)
        def _():
            lat_recv(inward, phase_lat)
            inward[band] = out[band]
            mine = inward.at[:, pl.ds(0, ROWS)]
            for k in range(1, NXC):
                remote(mine, of(mem), phase_chip, {"mem_0": (x + k) % NXC}).start()
            remote(mine, of(mem), phase_pair, partner).start()
            every[mem] = inward[...]
            wait_bytes(chips(GROUPS - 1), recv_sem.at[phase_chip])

        @pl.when(mem >= TILES)
        def _():
            wait_bytes(chips(GROUPS), recv_sem.at[phase_chip])

        for g in range(GROUPS):

            @pl.when(x != g)
            def _():
                there = g * NC + c
                remote(of(there), of(there), phase_pair, partner).start()

        wait_bytes(chips(GROUPS), recv_sem.at[phase_pair])

    def owner_schur(every):
        for t in range(TILES):
            cols = slice(t * TILE, (t + 1) * TILE)
            product = recv_p[:, :, cols].astype(F32) * every[t].astype(F32)
            flat[:, cols] = product.astype(BF).reshape(WIDE, TILE)

    def correlate(target, then=None):
        def lat(s, carry):
            rows = dot(lat_tab[s], flat[...]).astype(BF)
            across[s, :, EDGE : EDGE + NX] = rows
            across[s, :, :EDGE] = rows[:, NX - EDGE :]
            across[s, :, EDGE + NX :] = rows[:, :EDGE]
            return carry

        lax.fori_loop(0, SCALES, lat, 0)
        for g in range(GROUPS):
            first = g * GROUP
            total = jnp.zeros((WIDE, GROUP), F32)
            for s in range(SCALES):
                window = across[s, :, first : first + GROUP + 2 * EDGE]
                total = total + sw_ref[s] * dot(window, lon_tab[s])
            target[:, :, first : first + GROUP] = total.astype(BF).reshape(LEV, PAD, GROUP)
            if then is not None:
                then(g)

    def mix(tables, source):
        flat[...] = source[...].reshape(WIDE, NX)
        return dot(tables[0], flat[...]) + dot(tables[1], flat[...])

    def build_perm():
        row, col = iota((WIDE, LINES), 0), iota((WIDE, LINES), 1)
        inner = row % PAD
        match = jnp.logical_and(inner < ROWS, inner * LEV + row // PAD == col)
        perm[...] = match.astype(F32).astype(BF)

    def build_tables():
        def lat(s, carry):
            row, col = iota((WIDE, WIDE), 0), iota((WIDE, WIDE), 1)
            valid = jnp.logical_and(row % PAD < ROWS, col % PAD < ROWS)
            gap = (row // PAD - col // PAD) * ROWS + row % PAD - col % PAD
            scaled = gap.astype(F32) / latlen_ref[s]
            lat_tab[s] = jnp.where(valid, jnp.exp(-0.5 * scaled * scaled), 0.0).astype(BF)
            return carry

        lax.fori_loop(0, SCALES, lat, 0)

        def lon(s, carry):
            tall = (GROUP + 2 * EDGE, GROUP)
            gap = iota(tall, 0) - EDGE - iota(tall, 1)
            scaled = gap.astype(F32) / lonlen_ref[s]
            lon_tab[s] = jnp.exp(-0.5 * scaled * scaled).astype(BF)
            return carry

        lax.fori_loop(0, SCALES, lon, 0)
        vert = vert_ref[...]
        both = lax.dot_general(
            vert,
            vert,
            (((1,), (1,)), ((), ())),
            precision=lax.Precision.HIGHEST,
            preferred_element_type=F32,
        )
        pick_row = (iota((LINES, LEV), 0) % LEV == iota((LINES, LEV), 1)).astype(F32).astype(BF)
        pick_col = (iota((LEV, WIDE), 1) // PAD == iota((LEV, WIDE), 0)).astype(F32).astype(BF)
        same = iota((LINES, WIDE), 0) // LEV == iota((LINES, WIDE), 1) % PAD
        for matrix, target in ((vert.T, grad_mix), (both, image_mix)):
            high = matrix.astype(BF)
            low = (matrix - high.astype(F32)).astype(BF)
            for index, piece in enumerate((high, low)):
                rows = dot(pick_row, piece).astype(BF)
                target[index] = jnp.where(same, -dot(rows, pick_col), 0.0).astype(BF)

    def pert():
        return pert_ref[...].astype(F32).reshape(LINES, NX)

    for buffer in (recv_p, recv_t, recv_u, recv_r):
        clear(buffer)
    for buffer in (tile_in, tile_in_two):
        clear(buffer)
    for every in (tiles, tiles_two):
        for t in range(TILES):
            clear(every.at[t])
    lane = iota((1, 128), 1)
    stats[...] = jnp.zeros((1, 128), F32)
    build_perm()
    scatter(spread, True)
    tile_out[...] = by_level(spread[...].astype(BF))
    pl.semaphore_wait(barrier, BANDS - 1 + MEMS - 1)

    @pl.when(mem < TILES)
    def _():
        lat_start(tile_out, tile_in, S1)

    send_p[...] = by_level(pert_ref[...].reshape(LINES, NX))
    lat_start(send_p, recv_p, PP)
    build_tables()
    tile_gather(tile_out, tile_in, tiles, S1, A1, B1)
    scatter(weight, False)
    recv_p[band] = send_p[band]
    lat_recv(recv_p, PP)
    owner_schur(tiles)
    correlate(send_t)
    lat_start(send_t, recv_t, TT, 0, EARLY)
    flat[...] = send_t[...].reshape(WIDE, NX)
    correlate(send_u, group_start(send_u, recv_u, UU))
    recv_u[band] = send_u[band]
    recv_t[band] = send_t[band]

    def image_step():
        part_in[mem] = part[mem]
        wait_bytes(part_in.at[pl.ds(0, MEMS - 1)], recv_sem.at[RS])
        image = jnp.sum(part_in[...].astype(F32), axis=0)
        weighted = weight[...] * image
        square = jnp.sum(weighted * image)
        first = -jnp.sum(spread[...] * image)
        stats[...] = jnp.where(lane == 0, first, jnp.where(lane == 1, square, 0.0))
        tile_out_two[...] = by_level(weighted.astype(BF))
        lat_start(tile_out_two, tile_in_two, S2)

    for g in range(GROUPS):
        cols = slice(g * GROUP, (g + 1) * GROUP)
        group_bytes(recv_u, g, recv_sem.at[UU + g])
        got = recv_u[:, :, cols].reshape(WIDE, GROUP)
        mixed = dot(image_mix[0], got) + dot(image_mix[1], got)
        partial = (pert_ref[:, :, cols].astype(F32).reshape(LINES, GROUP) * mixed).astype(BF)
        for half in range(NC):
            t = g * NC + half
            part[t] = partial[:, half * TILE : (half + 1) * TILE]

            @pl.when(mem != t)
            def _():
                to = {"mem_0": g, "mem_1": half}
                remote(part.at[t], part_in.at[mem], RS, to).start()

        if g > 0:
            pl.when(x == g - 1)(image_step)

    @pl.when(x == GROUPS - 1)
    def _():
        lat_start(send_t, recv_t, TT, EARLY, NEAR)
        image_step()
        lat_start(send_t, recv_t, TT, NEAR, TAIL)

    @pl.when(x != GROUPS - 1)
    def _():
        lat_start(send_t, recv_t, TT, EARLY, TAIL)

    tile_gather(tile_out_two, tile_in_two, tiles_two, S2, A2, B2)
    owner_schur(tiles_two)
    correlate(send_r, group_start(send_r, recv_r, RR))
    lat_start(send_t, recv_t, TT, TAIL, BANDS - 1)
    recv_r[band] = send_r[band]
    hess_square = 0.0
    for g in range(GROUPS):
        cols = slice(g * GROUP, (g + 1) * GROUP)
        group_bytes(recv_r, g, recv_sem.at[RR + g])
        got = recv_r[:, :, cols].reshape(WIDE, GROUP)
        hess = -(dot(grad_mix[0], got) + dot(grad_mix[1], got))
        h_ref[:, cols] = hess
        hess_square = hess_square + jnp.sum(hess * hess)
    row = jnp.where(lane == 2, hess_square, stats[...])
    keep_h = pltpu.make_async_copy(h_ref, h_out, out_sem.at[1])
    row_mem[...] = row

    def tell_mem(k, carry):
        _, to = mem_peer(k)
        remote(row_mem, sums_mem.at[mem], SM, to).start()
        return carry

    lax.fori_loop(1, MEMS, tell_mem, 0)
    sums_mem[mem] = row
    wait_bytes(sums_mem.at[pl.ds(0, MEMS - 1)], recv_sem.at[SM])
    row = jnp.sum(sums_mem[...], axis=0)
    row_lat[...] = row

    def tell_lat(k, carry):
        _, to = lat_peer(k)
        remote(row_lat, sums_lat.at[band], SL, to).start()
        return carry

    lax.fori_loop(0, BANDS - 1, tell_lat, 0)
    sums_lat[band] = row
    keep_h.start()
    lat_recv(recv_t, TT)
    f_ref[...] = mix(grad_mix, recv_t)
    keep_f = pltpu.make_async_copy(f_ref, f_out, out_sem.at[0])
    keep_f.start()
    wait_bytes(sums_lat.at[pl.ds(0, BANDS - 1)], recv_sem.at[SL])
    total = jnp.sum(sums_lat[...], axis=0)
    grad_square, obs_square, hess_square = (
        jnp.sum(jnp.where(lane == index, total, 0.0)) for index in range(3)
    )
    first_step = grad_square / (grad_square + obs_square)
    second_step = (grad_square + obs_square) / (grad_square + 2.0 * obs_square + hess_square)
    first_ref[...] = jnp.full((PAD, NX), first_step, F32)
    second_ref[...] = jnp.full((PAD, NX), second_step, F32)
    keep_f.wait()
    keep_h.wait()

    for buffer, phase in ((send_p, PP), (send_t, TT)):
        lat_sent(buffer, phase)
    for g in range(GROUPS):
        group_bytes(send_u, g, send_sem.at[UU + g])
        group_bytes(send_r, g, send_sem.at[RR + g])

    @pl.when(mem < TILES)
    def _():
        lat_sent(tile_out, S1)
        lat_sent(tile_out_two, S2)
        for every, phase in ((tiles, A1), (tiles_two, A2)):
            wait_bytes(every.at[pl.ds(0, NXC - 1), :, pl.ds(0, ROWS)], send_sem.at[phase])
        wait_bytes(part_in.at[pl.ds(0, TILES - 1)], send_sem.at[RS])

    for every, phase in ((tiles, B1), (tiles_two, B2)):
        wait_bytes(every.at[pl.ds(0, GROUPS), :, pl.ds(0, ROWS)], send_sem.at[phase])

    @pl.when(mem >= TILES)
    def _():
        wait_bytes(part_in.at[pl.ds(0, TILES)], send_sem.at[RS])

    wait_bytes(sums_mem.at[pl.ds(0, MEMS - 1)], send_sem.at[SM])
    wait_bytes(sums_lat.at[pl.ds(0, BANDS - 1)], send_sem.at[SL])


def finish(f_ref, h_ref, first_ref, second_ref, control_ref, gradient_ref):
    first_step, second_step = first_ref[0:1, :], second_ref[0:1, :]
    gradient = f_ref[...] - first_step * (f_ref[...] + h_ref[...])
    gradient_ref[...] = gradient
    control_ref[...] = -first_step * f_ref[...] - second_step * gradient


def local(
    ens_perts,
    vert_loc,
    lat_lengths,
    lon_lengths,
    scale_weights,
    obs_cell,
    obs_accept,
    innovation,
    obs_precision,
):
    vmem = pl.BlockSpec(memory_space=pltpu.VMEM)
    smem = pl.BlockSpec(memory_space=pltpu.SMEM)
    hbm = pl.BlockSpec(memory_space=pl.ANY)
    slab = pltpu.VMEM((BANDS, PAD, NX), BF)
    lines = pltpu.VMEM((LINES, NX), F32)
    chunk = pltpu.VMEM((LINES, TILE), F32)
    level_tile = pltpu.VMEM((BANDS, PAD, TILE), BF)
    all_tiles = pltpu.VMEM((MEMS, BANDS, PAD, TILE), BF)
    grad, hess, first_step, second_step = pl.pallas_call(
        kernel,
        out_shape=(
            jax.ShapeDtypeStruct((LINES, NX), F32),
            jax.ShapeDtypeStruct((LINES, NX), F32),
            jax.ShapeDtypeStruct((PAD, NX), F32),
            jax.ShapeDtypeStruct((PAD, NX), F32),
        ),
        in_specs=[vmem, vmem, smem, smem, smem, vmem, vmem, vmem, vmem],
        out_specs=(hbm, hbm, vmem, vmem),
        scratch_shapes=[
            pltpu.VMEM((WIDE, LINES), BF),
            pltpu.VMEM((SCALES, WIDE, WIDE), BF),
            pltpu.VMEM((SCALES, GROUP + 2 * EDGE, GROUP), BF),
            pltpu.VMEM((2, LINES, WIDE), BF),
            pltpu.VMEM((2, LINES, WIDE), BF),
            pltpu.VMEM((1, OBS), jnp.int32),
            pltpu.VMEM((1, OBS), jnp.int32),
            chunk,
            chunk,
            pltpu.VMEM((SCALES, WIDE, NX + 2 * EDGE), BF),
            pltpu.VMEM((WIDE, NX), BF),
            slab,
            slab,
            slab,
            slab,
            slab,
            slab,
            slab,
            slab,
            level_tile,
            level_tile,
            all_tiles,
            level_tile,
            level_tile,
            all_tiles,
            pltpu.VMEM((TILES, LINES, TILE), BF),
            pltpu.VMEM((MEMS, LINES, TILE), BF),
            lines,
            lines,
            pltpu.VMEM((1, 128), F32),
            pltpu.VMEM((1, 128), F32),
            pltpu.VMEM((1, 128), F32),
            pltpu.VMEM((MEMS, 1, 128), F32),
            pltpu.VMEM((BANDS, 1, 128), F32),
            pltpu.SemaphoreType.DMA((11 + 2 * GROUPS,)),
            pltpu.SemaphoreType.DMA((11 + 2 * GROUPS,)),
            pltpu.SemaphoreType.DMA((2,)),
        ],
        compiler_params=pltpu.CompilerParams(
            collective_id=0, has_side_effects=True, vmem_limit_bytes=62 * 1024 * 1024
        ),
    )(
        ens_perts[0].transpose(1, 0, 2),
        vert_loc,
        lat_lengths,
        lon_lengths,
        scale_weights,
        obs_cell.reshape(1, OBS),
        obs_accept.reshape(1, OBS),
        innovation.reshape(1, OBS),
        obs_precision.reshape(1, OBS),
    )
    block = pl.BlockSpec((2 * LEV, NX), lambda i: (i, 0))
    whole = pl.BlockSpec((PAD, NX), lambda i: (0, 0))
    new_control, gradient = pl.pallas_call(
        finish,
        out_shape=(
            jax.ShapeDtypeStruct((LINES, NX), F32),
            jax.ShapeDtypeStruct((LINES, NX), F32),
        ),
        grid=(LINES // (2 * LEV),),
        in_specs=[block, block, whole, whole],
        out_specs=(block, block),
        compiler_params=pltpu.CompilerParams(vmem_limit_bytes=62 * 1024 * 1024),
    )(grad, hess, first_step, second_step)

    def placed(field):
        return field.reshape(ROWS, LEV, NX).transpose(1, 0, 2)[None]

    return (placed(new_control), placed(gradient))


def solution(mesh):
    split = Mesh(mesh.devices.reshape(NZ, NYC, NXC, NC), ("lat_0", "lat_1", "mem_0", "mem_1"))
    placed = (P(MEM, None, LAT, None), P(), P(), P(), P(), P(LAT), P(LAT), P(LAT), P(LAT))
    return jax.shard_map(
        local,
        mesh=split,
        in_specs=placed,
        out_specs=(P(MEM, None, LAT, None), P(MEM, None, LAT, None)),
        check_vma=False,
    )
```

```python
import jax
import jax.numpy as jnp
from jax import lax
from jax.experimental import pallas as pl
from jax.experimental.pallas import tpu as pltpu
from jax.sharding import Mesh
from jax.sharding import PartitionSpec as P

LAT = ("lat_0", "lat_1")
MEM = ("mem_0", "mem_1")
MESH_ID = pl.DeviceIdType.MESH
NZ, NYC, NXC, NC = 16, 4, 4, 2
BANDS = NZ * NYC
MEMS = NXC * NC
LEV = 64
ROWS = 6
PAD = 8
NX = 768
LINES = ROWS * LEV
WIDE = LEV * PAD
SCALES = 3
OBS = 8192
EDGE = 128
TILE = 128
TILES = NX // TILE
GROUP = 256
GROUPS = NX // GROUP
EARLY = 2
NEAR = 7
TAIL = 37
CHUNK = 512
BF = jnp.bfloat16
F32 = jnp.float32

PP, S1, A1, B1, TT, RS, S2, A2, B2, SM, SL, UU = range(12)
RR = UU + 3


def iota(shape, dim):
    return lax.broadcasted_iota(jnp.int32, shape, dim)


def dot(a, b):
    return jnp.dot(a, b, preferred_element_type=F32)


def kernel(
    pert_ref,
    vert_ref,
    latlen_ref,
    lonlen_ref,
    sw_ref,
    cell_ref,
    accept_ref,
    innov_ref,
    prec_ref,
    f_out,
    h_out,
    first_ref,
    second_ref,
    perm,
    lat_tab,
    lon_tab,
    grad_mix,
    image_mix,
    line_ref,
    col_ref,
    spread,
    weight,
    across,
    flat,
    send_p,
    send_t,
    send_u,
    send_r,
    recv_p,
    recv_t,
    recv_u,
    recv_r,
    tile_out,
    tile_in,
    tiles,
    tile_out_two,
    tile_in_two,
    tiles_two,
    part,
    part_in,
    f_ref,
    h_ref,
    stats,
    row_mem,
    row_lat,
    sums_mem,
    sums_lat,
    send_sem,
    recv_sem,
    out_sem,
):
    z = lax.axis_index("lat_0")
    y = lax.axis_index("lat_1")
    x = lax.axis_index("mem_0")
    c = lax.axis_index("mem_1")
    band = z * NYC + y
    mem = x * NC + c

    def lat_peer(k):
        j = k // NYC
        dz = NZ // 2 + ((j + 1) // 2) * (1 - 2 * (j % 2))
        zz = (z + dz) % NZ
        yy = (y + (NYC - 1) - k % NYC) % NYC
        return zz * NYC + yy, {"lat_0": zz, "lat_1": yy}

    def mem_peer(k):
        other = (mem + k) % MEMS
        return other, {"mem_0": other // NC, "mem_1": other % NC}

    barrier = pltpu.get_barrier_semaphore()

    def greet_lat(k, carry):
        pl.semaphore_signal(barrier, inc=1, device_id=lat_peer(k)[1], device_id_type=MESH_ID)
        return carry

    def greet_mem(k, carry):
        pl.semaphore_signal(barrier, inc=1, device_id=mem_peer(k)[1], device_id_type=MESH_ID)
        return carry

    lax.fori_loop(0, BANDS - 1, greet_lat, 0)
    lax.fori_loop(1, MEMS, greet_mem, 0)

    def remote(src, dst, phase, to):
        return pltpu.make_async_remote_copy(
            src_ref=src,
            dst_ref=dst,
            send_sem=send_sem.at[phase],
            recv_sem=recv_sem.at[phase],
            device_id=to,
            device_id_type=MESH_ID,
        )

    def lat_start(src, dst, phase, first=0, last=BANDS - 1):
        def go(k, carry):
            there, to = lat_peer(k)
            remote(src.at[there, pl.ds(0, ROWS)], dst.at[band, pl.ds(0, ROWS)], phase, to).start()
            return carry

        lax.fori_loop(first, last, go, 0)

    def group_start(src, dst, phase):
        def start(g):
            cols = pl.ds(g * GROUP, GROUP)

            def go(k, carry):
                there, to = lat_peer(k)
                here = src.at[there, pl.ds(0, ROWS), cols]
                remote(here, dst.at[band, pl.ds(0, ROWS), cols], phase + g, to).start()
                return carry

            lax.fori_loop(0, BANDS - 1, go, 0)

        return start

    def group_bytes(ref, g, sem):
        cols = pl.ds(g * GROUP, GROUP)
        wait_bytes(ref.at[pl.ds(0, BANDS - 1), pl.ds(0, ROWS), cols], sem)

    def wait_bytes(ref, sem):
        pltpu.make_async_copy(ref, ref, sem).wait()

    def lat_recv(dst, phase):
        wait_bytes(dst.at[pl.ds(0, BANDS - 1), pl.ds(0, ROWS)], recv_sem.at[phase])

    def lat_sent(src, phase):
        wait_bytes(src.at[pl.ds(0, BANDS - 1), pl.ds(0, ROWS)], send_sem.at[phase])

    def clear(buffer):
        shape = (BANDS, PAD - ROWS, buffer.shape[-1])
        buffer[:, ROWS:PAD, :] = jnp.zeros(shape, BF)

    cell = cell_ref[...]
    line = ((cell.astype(F32) + 0.5) * (1.0 / NX)).astype(jnp.int32)
    level = ((line.astype(F32) + 0.5) * (1.0 / ROWS)).astype(jnp.int32)
    col_ref[...] = cell - line * NX - mem * TILE
    line_ref[...] = (line - level * ROWS) * LEV + level

    def scatter(target, with_innovation):
        target[...] = jnp.zeros((LINES, TILE), F32)

        def step(k, carry):
            here = pl.ds(pl.multiple_of(k * CHUNK, CHUNK), CHUNK)
            values = accept_ref[:, here].astype(F32) * prec_ref[:, here]
            if with_innovation:
                values = values * innov_ref[:, here]
            high = values.astype(BF).astype(F32)
            at_line = iota((LINES, CHUNK), 0) == line_ref[:, here]
            at_col = (iota((TILE, CHUNK), 0) == col_ref[:, here]).astype(F32).astype(BF)
            total = target[...]
            for piece in (high,) if with_innovation else (high, values - high):
                picked = jnp.where(at_line, piece, 0.0).astype(BF)
                total = total + lax.dot_general(
                    picked, at_col, (((1,), (1,)), ((), ())), preferred_element_type=F32
                )
            target[...] = total
            return carry

        lax.fori_loop(0, OBS // CHUNK, step, 0)

    def by_level(values):
        return dot(perm[...], values).astype(BF).reshape(LEV, PAD, values.shape[-1])

    def tile_gather(out, inward, every, phase_lat, phase_chip, phase_pair):
        partner = {"mem_1": 1 - c}

        def of(tile):
            return every.at[tile, :, pl.ds(0, ROWS)]

        def chips(count):
            return every.at[pl.ds(0, count), :, pl.ds(0, ROWS)]

        @pl.when(mem < TILES)
        def _():
            lat_recv(inward, phase_lat)
            inward[band] = out[band]
            mine = inward.at[:, pl.ds(0, ROWS)]
            for k in range(1, NXC):
                remote(mine, of(mem), phase_chip, {"mem_0": (x + k) % NXC}).start()
            remote(mine, of(mem), phase_pair, partner).start()
            every[mem] = inward[...]
            wait_bytes(chips(GROUPS - 1), recv_sem.at[phase_chip])

        @pl.when(mem >= TILES)
        def _():
            wait_bytes(chips(GROUPS), recv_sem.at[phase_chip])

        for g in range(GROUPS):

            @pl.when(x != g)
            def _():
                there = g * NC + c
                remote(of(there), of(there), phase_pair, partner).start()

        wait_bytes(chips(GROUPS), recv_sem.at[phase_pair])

    def owner_schur(every):
        for t in range(TILES):
            cols = slice(t * TILE, (t + 1) * TILE)
            product = recv_p[:, :, cols].astype(F32) * every[t].astype(F32)
            flat[:, cols] = product.astype(BF).reshape(WIDE, TILE)

    def correlate(target, then=None):
        def lat(s, carry):
            rows = dot(lat_tab[s], flat[...]).astype(BF)
            across[s, :, EDGE : EDGE + NX] = rows
            across[s, :, :EDGE] = rows[:, NX - EDGE :]
            across[s, :, EDGE + NX :] = rows[:, :EDGE]
            return carry

        lax.fori_loop(0, SCALES, lat, 0)
        for g in range(GROUPS):
            first = g * GROUP
            total = jnp.zeros((WIDE, GROUP), F32)
            for s in range(SCALES):
                window = across[s, :, first : first + GROUP + 2 * EDGE]
                total = total + sw_ref[s] * dot(window, lon_tab[s])
            target[:, :, first : first + GROUP] = total.astype(BF).reshape(LEV, PAD, GROUP)
            if then is not None:
                then(g)

    def mix(tables, source):
        flat[...] = source[...].reshape(WIDE, NX)
        return dot(tables[0], flat[...]) + dot(tables[1], flat[...])

    def build_perm():
        row, col = iota((WIDE, LINES), 0), iota((WIDE, LINES), 1)
        inner = row % PAD
        match = jnp.logical_and(inner < ROWS, inner * LEV + row // PAD == col)
        perm[...] = match.astype(F32).astype(BF)

    def build_tables():
        def lat(s, carry):
            row, col = iota((WIDE, WIDE), 0), iota((WIDE, WIDE), 1)
            valid = jnp.logical_and(row % PAD < ROWS, col % PAD < ROWS)
            gap = (row // PAD - col // PAD) * ROWS + row % PAD - col % PAD
            scaled = gap.astype(F32) / latlen_ref[s]
            lat_tab[s] = jnp.where(valid, jnp.exp(-0.5 * scaled * scaled), 0.0).astype(BF)
            return carry

        lax.fori_loop(0, SCALES, lat, 0)

        def lon(s, carry):
            tall = (GROUP + 2 * EDGE, GROUP)
            gap = iota(tall, 0) - EDGE - iota(tall, 1)
            scaled = gap.astype(F32) / lonlen_ref[s]
            lon_tab[s] = jnp.exp(-0.5 * scaled * scaled).astype(BF)
            return carry

        lax.fori_loop(0, SCALES, lon, 0)
        vert = vert_ref[...]
        both = lax.dot_general(
            vert,
            vert,
            (((1,), (1,)), ((), ())),
            precision=lax.Precision.HIGHEST,
            preferred_element_type=F32,
        )
        pick_row = (iota((LINES, LEV), 0) % LEV == iota((LINES, LEV), 1)).astype(F32).astype(BF)
        pick_col = (iota((LEV, WIDE), 1) // PAD == iota((LEV, WIDE), 0)).astype(F32).astype(BF)
        same = iota((LINES, WIDE), 0) // LEV == iota((LINES, WIDE), 1) % PAD
        for matrix, target in ((vert.T, grad_mix), (both, image_mix)):
            high = matrix.astype(BF)
            low = (matrix - high.astype(F32)).astype(BF)
            for index, piece in enumerate((high, low)):
                rows = dot(pick_row, piece).astype(BF)
                target[index] = jnp.where(same, -dot(rows, pick_col), 0.0).astype(BF)

    def pert():
        return pert_ref[...].astype(F32).reshape(LINES, NX)

    for buffer in (recv_p, recv_t, recv_u, recv_r):
        clear(buffer)
    for buffer in (tile_in, tile_in_two):
        clear(buffer)
    for every in (tiles, tiles_two):
        for t in range(TILES):
            clear(every.at[t])
    lane = iota((1, 128), 1)
    stats[...] = jnp.zeros((1, 128), F32)
    build_perm()
    scatter(spread, True)
    tile_out[...] = by_level(spread[...].astype(BF))
    pl.semaphore_wait(barrier, BANDS - 1 + MEMS - 1)

    @pl.when(mem < TILES)
    def _():
        lat_start(tile_out, tile_in, S1)

    send_p[...] = by_level(pert_ref[...].reshape(LINES, NX))
    lat_start(send_p, recv_p, PP)
    build_tables()
    tile_gather(tile_out, tile_in, tiles, S1, A1, B1)
    scatter(weight, False)
    recv_p[band] = send_p[band]
    lat_recv(recv_p, PP)
    owner_schur(tiles)
    correlate(send_t)
    lat_start(send_t, recv_t, TT, 0, EARLY)
    flat[...] = send_t[...].reshape(WIDE, NX)
    correlate(send_u, group_start(send_u, recv_u, UU))
    recv_u[band] = send_u[band]
    recv_t[band] = send_t[band]

    def image_step():
        part_in[mem] = part[mem]
        wait_bytes(part_in.at[pl.ds(0, MEMS - 1)], recv_sem.at[RS])
        image = jnp.sum(part_in[...].astype(F32), axis=0)
        weighted = weight[...] * image
        square = jnp.sum(weighted * image)
        first = -jnp.sum(spread[...] * image)
        stats[...] = jnp.where(lane == 0, first, jnp.where(lane == 1, square, 0.0))
        tile_out_two[...] = by_level(weighted.astype(BF))
        lat_start(tile_out_two, tile_in_two, S2)

    for g in range(GROUPS):
        cols = slice(g * GROUP, (g + 1) * GROUP)
        group_bytes(recv_u, g, recv_sem.at[UU + g])
        got = recv_u[:, :, cols].reshape(WIDE, GROUP)
        mixed = dot(image_mix[0], got) + dot(image_mix[1], got)
        partial = (pert_ref[:, :, cols].astype(F32).reshape(LINES, GROUP) * mixed).astype(BF)
        for half in range(NC):
            t = g * NC + half
            part[t] = partial[:, half * TILE : (half + 1) * TILE]

            @pl.when(mem != t)
            def _():
                to = {"mem_0": g, "mem_1": half}
                remote(part.at[t], part_in.at[mem], RS, to).start()

        if g > 0:
            pl.when(x == g - 1)(image_step)

    @pl.when(x == GROUPS - 1)
    def _():
        lat_start(send_t, recv_t, TT, EARLY, NEAR)
        image_step()
        lat_start(send_t, recv_t, TT, NEAR, TAIL)

    @pl.when(x != GROUPS - 1)
    def _():
        lat_start(send_t, recv_t, TT, EARLY, TAIL)

    tile_gather(tile_out_two, tile_in_two, tiles_two, S2, A2, B2)
    owner_schur(tiles_two)
    correlate(send_r, group_start(send_r, recv_r, RR))
    lat_start(send_t, recv_t, TT, TAIL, BANDS - 1)
    recv_r[band] = send_r[band]
    hess_square = 0.0
    for g in range(GROUPS):
        cols = slice(g * GROUP, (g + 1) * GROUP)
        group_bytes(recv_r, g, recv_sem.at[RR + g])
        got = recv_r[:, :, cols].reshape(WIDE, GROUP)
        hess = -(dot(grad_mix[0], got) + dot(grad_mix[1], got))
        h_ref[:, cols] = hess
        hess_square = hess_square + jnp.sum(hess * hess)
    row = jnp.where(lane == 2, hess_square, stats[...])
    keep_h = pltpu.make_async_copy(h_ref, h_out, out_sem.at[1])
    row_mem[...] = row

    def tell_mem(k, carry):
        _, to = mem_peer(k)
        remote(row_mem, sums_mem.at[mem], SM, to).start()
        return carry

    lax.fori_loop(1, MEMS, tell_mem, 0)
    sums_mem[mem] = row
    wait_bytes(sums_mem.at[pl.ds(0, MEMS - 1)], recv_sem.at[SM])
    row = jnp.sum(sums_mem[...], axis=0)
    row_lat[...] = row

    def tell_lat(k, carry):
        _, to = lat_peer(k)
        remote(row_lat, sums_lat.at[band], SL, to).start()
        return carry

    lax.fori_loop(0, BANDS - 1, tell_lat, 0)
    sums_lat[band] = row
    keep_h.start()
    lat_recv(recv_t, TT)
    f_ref[...] = mix(grad_mix, recv_t)
    keep_f = pltpu.make_async_copy(f_ref, f_out, out_sem.at[0])
    keep_f.start()
    wait_bytes(sums_lat.at[pl.ds(0, BANDS - 1)], recv_sem.at[SL])
    total = jnp.sum(sums_lat[...], axis=0)
    grad_square, obs_square, hess_square = (
        jnp.sum(jnp.where(lane == index, total, 0.0)) for index in range(3)
    )
    first_step = grad_square / (grad_square + obs_square)
    second_step = (grad_square + obs_square) / (grad_square + 2.0 * obs_square + hess_square)
    first_ref[...] = jnp.full((PAD, NX), first_step, F32)
    second_ref[...] = jnp.full((PAD, NX), second_step, F32)
    keep_f.wait()
    keep_h.wait()

    for buffer, phase in ((send_p, PP), (send_t, TT)):
        lat_sent(buffer, phase)
    for g in range(GROUPS):
        group_bytes(send_u, g, send_sem.at[UU + g])
        group_bytes(send_r, g, send_sem.at[RR + g])

    @pl.when(mem < TILES)
    def _():
        lat_sent(tile_out, S1)
        lat_sent(tile_out_two, S2)
        for every, phase in ((tiles, A1), (tiles_two, A2)):
            wait_bytes(every.at[pl.ds(0, NXC - 1), :, pl.ds(0, ROWS)], send_sem.at[phase])
        wait_bytes(part_in.at[pl.ds(0, TILES - 1)], send_sem.at[RS])

    for every, phase in ((tiles, B1), (tiles_two, B2)):
        wait_bytes(every.at[pl.ds(0, GROUPS), :, pl.ds(0, ROWS)], send_sem.at[phase])

    @pl.when(mem >= TILES)
    def _():
        wait_bytes(part_in.at[pl.ds(0, TILES)], send_sem.at[RS])

    wait_bytes(sums_mem.at[pl.ds(0, MEMS - 1)], send_sem.at[SM])
    wait_bytes(sums_lat.at[pl.ds(0, BANDS - 1)], send_sem.at[SL])


def finish(f_ref, h_ref, first_ref, second_ref, control_ref, gradient_ref):
    first_step, second_step = first_ref[0:1, :], second_ref[0:1, :]
    gradient = f_ref[...] - first_step * (f_ref[...] + h_ref[...])
    gradient_ref[...] = gradient
    control_ref[...] = -first_step * f_ref[...] - second_step * gradient


def local(
    ens_perts,
    vert_loc,
    lat_lengths,
    lon_lengths,
    scale_weights,
    obs_cell,
    obs_accept,
    innovation,
    obs_precision,
):
    vmem = pl.BlockSpec(memory_space=pltpu.VMEM)
    smem = pl.BlockSpec(memory_space=pltpu.SMEM)
    hbm = pl.BlockSpec(memory_space=pl.ANY)
    slab = pltpu.VMEM((BANDS, PAD, NX), BF)
    lines = pltpu.VMEM((LINES, NX), F32)
    chunk = pltpu.VMEM((LINES, TILE), F32)
    level_tile = pltpu.VMEM((BANDS, PAD, TILE), BF)
    all_tiles = pltpu.VMEM((MEMS, BANDS, PAD, TILE), BF)
    grad, hess, first_step, second_step = pl.pallas_call(
        kernel,
        out_shape=(
            jax.ShapeDtypeStruct((LINES, NX), F32),
            jax.ShapeDtypeStruct((LINES, NX), F32),
            jax.ShapeDtypeStruct((PAD, NX), F32),
            jax.ShapeDtypeStruct((PAD, NX), F32),
        ),
        in_specs=[vmem, vmem, smem, smem, smem, vmem, vmem, vmem, vmem],
        out_specs=(hbm, hbm, vmem, vmem),
        scratch_shapes=[
            pltpu.VMEM((WIDE, LINES), BF),
            pltpu.VMEM((SCALES, WIDE, WIDE), BF),
            pltpu.VMEM((SCALES, GROUP + 2 * EDGE, GROUP), BF),
            pltpu.VMEM((2, LINES, WIDE), BF),
            pltpu.VMEM((2, LINES, WIDE), BF),
            pltpu.VMEM((1, OBS), jnp.int32),
            pltpu.VMEM((1, OBS), jnp.int32),
            chunk,
            chunk,
            pltpu.VMEM((SCALES, WIDE, NX + 2 * EDGE), BF),
            pltpu.VMEM((WIDE, NX), BF),
            slab,
            slab,
            slab,
            slab,
            slab,
            slab,
            slab,
            slab,
            level_tile,
            level_tile,
            all_tiles,
            level_tile,
            level_tile,
            all_tiles,
            pltpu.VMEM((TILES, LINES, TILE), BF),
            pltpu.VMEM((MEMS, LINES, TILE), BF),
            lines,
            lines,
            pltpu.VMEM((1, 128), F32),
            pltpu.VMEM((1, 128), F32),
            pltpu.VMEM((1, 128), F32),
            pltpu.VMEM((MEMS, 1, 128), F32),
            pltpu.VMEM((BANDS, 1, 128), F32),
            pltpu.SemaphoreType.DMA((11 + 2 * GROUPS,)),
            pltpu.SemaphoreType.DMA((11 + 2 * GROUPS,)),
            pltpu.SemaphoreType.DMA((2,)),
        ],
        compiler_params=pltpu.CompilerParams(
            collective_id=0, has_side_effects=True, vmem_limit_bytes=62 * 1024 * 1024
        ),
    )(
        ens_perts[0].transpose(1, 0, 2),
        vert_loc,
        lat_lengths,
        lon_lengths,
        scale_weights,
        obs_cell.reshape(1, OBS),
        obs_accept.reshape(1, OBS),
        innovation.reshape(1, OBS),
        obs_precision.reshape(1, OBS),
    )
    block = pl.BlockSpec((2 * LEV, NX), lambda i: (i, 0))
    whole = pl.BlockSpec((PAD, NX), lambda i: (0, 0))
    new_control, gradient = pl.pallas_call(
        finish,
        out_shape=(
            jax.ShapeDtypeStruct((LINES, NX), F32),
            jax.ShapeDtypeStruct((LINES, NX), F32),
        ),
        grid=(LINES // (2 * LEV),),
        in_specs=[block, block, whole, whole],
        out_specs=(block, block),
        compiler_params=pltpu.CompilerParams(vmem_limit_bytes=62 * 1024 * 1024),
    )(grad, hess, first_step, second_step)

    def placed(field):
        return field.reshape(ROWS, LEV, NX).transpose(1, 0, 2)[None]

    return (placed(new_control), placed(gradient))


def solution(mesh):
    split = Mesh(mesh.devices.reshape(NZ, NYC, NXC, NC), ("lat_0", "lat_1", "mem_0", "mem_1"))
    placed = (P(MEM, None, LAT, None), P(), P(), P(), P(), P(LAT), P(LAT), P(LAT), P(LAT))
    return jax.shard_map(
        local,
        mesh=split,
        in_specs=placed,
        out_specs=(P(MEM, None, LAT, None), P(MEM, None, LAT, None)),
        check_vma=False,
    )
```
